32 devices in a mesh: tower: 2 (over core), batch: 2 (over x), mp: 8 (over z, y).
Axes of the slice: x: 2, y: 2, z: 4, core: 2. Of those that a mesh axis runs over, the one named last changes fastest.
Arguments:
- acts: bfloat16 [2, 6144, 9216], P('tower', ('batch', 'mp')), may hold values from -6 to 6
- fc_weight: bfloat16 [2, 9216, 4096], P('tower', None, 'mp'), may hold values from -0.0625 to 0.0625
- fc_bias: bfloat16 [2, 4096], P('tower', 'mp'), may hold values from -3 to 3
- stitch: float32 [2, 2, 4096], P('tower', None, 'mp'), may hold values from 0.2 to 1
- image_grad: bfloat16 [2, 2048, 4096], P('tower', 'batch', 'mp'), may hold values from -8 to 8
- crop_counts: int32 [2048], P('batch'), may hold values from 1 to 3
- row_image: int32 [6144], P('batch'), may hold values from 0 to 2047, as said below
- row_live: int32 [6144], P('batch'), may hold values from 0 to 1, as said below
Outputs:
- stitched_out: bfloat16 [2, 6144, 4096], P('tower', 'batch', 'mp')
- acts_grad: bfloat16 [2, 6144, 9216], P('tower', ('batch', 'mp'))
- weight_grad: float32 [2, 9216, 4096], P('tower', None, 'mp')
- bias_grad: float32 [2, 4096], P('tower', 'mp')
- stitch_grad: float32 [2, 2, 4096], P('tower', None, 'mp')
The draws below stay inside these ranges and needn't reach their ends.
Inputs may be any that keep to these rules, and one draw needn't show every extreme that they name: `row_image`: each image's crop rows are consecutive slots of the 3072 slots of its index of batch, images in order; image i lies in batch block i // 1024; crop_counts[i] is the number of live rows of image i; every batch block has padding rows at its end, and padding rows name an image of their own block. `row_live`: live rows come first in each block of 3072 slots.
All inputs are finite; a program needn't handle non-finite values.
Results may differ from the reference program's by a relative error of at most 0.008.
Values may be sent and summed in bfloat16 or wider, within the bound.
No kernel may reach another device: no remote copies, remote signals or barrier semaphores. Data moves between devices by JAX's collectives and lax.ppermute only.
A program may use at most 320 MiB of HBM per device.

```python
import jax
import jax.numpy as jnp
from jax import lax

D_IN = 9216
F = 4096
ROW_DEV = 3072
IMAGES_PER_SLOT = 1024
ROWS = 6144
IMAGES = 2048


def layout_draw(key):
    base_key = jax.random.fold_in(key, 4711)
    first, second, third = jax.random.split(base_key, 3)
    blocks = IMAGES // IMAGES_PER_SLOT
    level = jax.random.randint(first, (blocks, 1), 0, 3)
    base = jax.random.randint(second, (blocks, IMAGES_PER_SLOT), 0, 2)
    extra = (jax.random.randint(third, (blocks, IMAGES_PER_SLOT), 0, 3) < level).astype(jnp.int32)
    counts = 1 + base + extra
    column = jnp.arange(IMAGES_PER_SLOT, dtype=jnp.int32)[None, :]
    counts = jnp.where(column == 0, 3, jnp.where(column == 1, 1, counts)).astype(jnp.int32)
    ends = jnp.cumsum(counts, axis=1)
    total = ends[:, -1]
    slots = jnp.arange(ROW_DEV, dtype=jnp.int32)
    local = jnp.sum((ends[:, None, :] <= slots[None, :, None]).astype(jnp.int32), axis=2)
    local = jnp.minimum(local, IMAGES_PER_SLOT - 1)
    images = local + jnp.arange(blocks, dtype=jnp.int32)[:, None] * IMAGES_PER_SLOT
    live = (slots[None, :] < total[:, None]).astype(jnp.int32)
    return (counts.reshape(-1), images.reshape(-1).astype(jnp.int32), live.reshape(-1))


def draw_crop_counts(key, part):
    return layout_draw(key)[0]


def draw_row_image(key, part):
    return layout_draw(key)[1]


def draw_row_live(key, part):
    return layout_draw(key)[2]


def steps_of(key, shape, pieces, low, high):
    factor_of, own = 1.0, jax.random.fold_in(key, 6)
    for axis_at, shards_of in pieces:
        heights = jnp.exp(jax.random.uniform(jax.random.fold_in(own, axis_at), (shards_of,), jnp.float32, low / len(pieces), high / len(pieces)))
        factor_of = factor_of * jnp.repeat(heights, shape[axis_at] // shards_of).reshape([-1 if axis == axis_at else 1 for axis in range(len(shape))])
    return factor_of


def scatter_about(stream_key, dims, scale, bound, cuts=(), held_as=jnp.bfloat16):
    values = jax.random.normal(stream_key, dims, jnp.float32) * scale
    if len(cuts) > 0:
        values = steps_of(stream_key, dims, cuts, -0.22, 0.18) * values
    return jnp.clip(values, min=-bound, max=bound).astype(held_as)


def setup_inputs(seed: int = 0) -> dict:
    arg_keys = jax.random.split(jax.random.key(seed), 9)
    return {
        "acts": scatter_about(arg_keys[0], (2, ROWS, D_IN), 1.0, 6.0, ((0, 2), (1, 16))),
        "fc_weight": scatter_about(arg_keys[1], (2, D_IN, F), D_IN ** -0.5, 0.0625, ((0, 2), (2, 8))),
        "fc_bias": scatter_about(arg_keys[2], (2, F), 0.5, 3.0, ((0, 2), (1, 8))),
        "stitch": jnp.clip(0.2 + 0.8 * jax.random.uniform(arg_keys[3], (2, 2, F), jnp.float32) ** steps_of(arg_keys[3], (2, 2, F), ((0, 2), (2, 8)), -0.2, 0.2), 0.2, 1.0),
        "image_grad": scatter_about(arg_keys[4], (2, IMAGES, F), 2.0, 8.0, ((0, 2), (1, 2), (2, 8))),
        "crop_counts": draw_crop_counts(jax.random.fold_in(arg_keys[8], 71), 0),
        "row_image": draw_row_image(jax.random.fold_in(arg_keys[8], 71), 0),
        "row_live": draw_row_live(jax.random.fold_in(arg_keys[8], 71), 0),
    }


@jax.custom_vjp
def lower_precision(v):
    return lax.optimization_barrier(v.astype(jnp.bfloat16)).astype(jnp.float32)

@jax.custom_vjp
def low_back(v):
    return v

def low_keep(v):
    return (lower_precision(v), None)

def low_pass(kept, grad):
    return (grad,)

def back_keep(v):
    return (v, None)

def back_low(kept, grad):
    return (lower_precision(grad),)
lower_precision.defvjp(low_keep, low_pass)
low_back.defvjp(back_keep, back_low)

def reference(acts, fc_weight, fc_bias, stitch, image_grad, crop_counts, row_image, row_live):
    live = row_live.astype(jnp.float32)
    per_row = jnp.take(crop_counts, row_image).astype(jnp.float32)
    row_weighting_scale = live / per_row

    def forward(feature_rows, weight_matrix, layer_bias, coefs):
        preactivation = jnp.einsum('zmc,zcy->zmy', lower_precision(feature_rows), lower_precision(weight_matrix), precision=lax.Precision.HIGHEST) + layer_bias[:, None, :]
        hidden = lower_precision(low_back(jax.nn.relu(preactivation)))
        stitched = coefs[:, 0, None, :] * hidden[0][None] + coefs[:, 1, None, :] * hidden[1][None]
        scaled = low_back(stitched) * row_weighting_scale[None, :, None]
        pooled = jax.vmap(lambda v: jax.ops.segment_sum(v, row_image, num_segments=IMAGES))(scaled)
        return (pooled, stitched)
    pooled, back_fn, stitched = jax.vjp(forward, acts.astype(jnp.float32), fc_weight.astype(jnp.float32), fc_bias.astype(jnp.float32), stitch, has_aux=True)
    grads = back_fn(image_grad.astype(jnp.float32))
    stitched_out = (stitched * live[None, :, None]).astype(jnp.bfloat16)
    return (stitched_out, grads[0].astype(jnp.bfloat16), grads[1], grads[2], grads[3])
```

```python
import jax
import jax.numpy as jnp
from jax import lax
from jax.sharding import PartitionSpec as P

BF = jnp.bfloat16
F32 = jnp.float32


def swapped(block, axis, mask):
    count = lax.axis_size(axis)
    return lax.ppermute(block, axis, [(i, i ^ mask) for i in range(count)])


def general(acts, fc_weight, fc_bias, stitch, image_grad, crop_counts, row_image, row_live):
    feature_rows = acts[0]
    weight_matrix = fc_weight[0]
    layer_bias = fc_bias[0].astype(jnp.float32)
    coefs = stitch[0]
    grads_img = image_grad[0]
    gathered = lax.all_gather(feature_rows, "mp", axis=0, tiled=True)
    preactivation = (
        jnp.dot(gathered, weight_matrix, preferred_element_type=jnp.float32) + layer_bias[None, :]
    )
    active = preactivation > 0
    hidden = jnp.maximum(preactivation, 0.0).astype(jnp.bfloat16)
    tower = lax.axis_index("tower")
    self_coefficient = jnp.where(tower == 0, coefs[0], coefs[1])
    other_coef = jnp.where(tower == 0, coefs[1], coefs[0])
    partner = swapped(hidden, "tower", 1)
    hidden_wide = hidden.astype(jnp.float32)
    partner_wide = partner.astype(jnp.float32)
    stitched = self_coefficient[None, :] * hidden_wide + other_coef[None, :] * partner_wide
    live = row_live.astype(jnp.float32)
    stitched_out = (stitched * live[:, None]).astype(jnp.bfloat16)
    img_dev = crop_counts.shape[0]
    local_img = row_image - lax.axis_index("batch") * img_dev
    match = local_img[:, None] == jnp.arange(img_dev, dtype=jnp.int32)[None, :]
    per_row = jnp.sum(jnp.where(match, crop_counts[None, :].astype(jnp.float32), 0.0), axis=1)
    row_weighting_scale = live / per_row
    picked = jnp.dot(match.astype(jnp.bfloat16), grads_img, preferred_element_type=jnp.float32)
    out_grad = (picked * row_weighting_scale[:, None]).astype(jnp.bfloat16)
    out_wide = out_grad.astype(jnp.float32)
    returned = swapped(other_coef[None, :] * out_wide, "tower", 1)
    hidden_grad = (self_coefficient[None, :] * out_wide + returned).astype(jnp.bfloat16)
    pre_grad = jnp.where(active, hidden_grad, jnp.zeros_like(hidden_grad))
    own_stitch = jnp.sum(out_wide * hidden_wide, axis=0)
    other_stitch = jnp.sum(out_wide * partner_wide, axis=0)
    stitch_grad = jnp.where(
        tower == 0, jnp.stack([own_stitch, other_stitch]), jnp.stack([other_stitch, own_stitch])
    )
    bias_grad = jnp.sum(pre_grad.astype(jnp.float32), axis=0)
    weight_grad = lax.dot_general(
        gathered, pre_grad, (((0,), (0,)), ((), ())), preferred_element_type=jnp.float32
    )
    weight_grad, bias_grad, stitch_grad = lax.psum((weight_grad, bias_grad, stitch_grad), "batch")
    input_grad = lax.psum_scatter(
        lax.dot_general(
            pre_grad, weight_matrix, (((1,), (1,)), ((), ())), preferred_element_type=jnp.float32
        ),
        "mp",
        scatter_dimension=0,
        tiled=True,
    )
    return (
        stitched_out[None],
        input_grad.astype(jnp.bfloat16)[None],
        weight_grad[None],
        bias_grad[None],
        stitch_grad[None],
    )


def squares(acts, fc_weight, fc_bias, stitch, image_grad, crop_counts, row_image, row_live):
    x = acts[0]
    w = fc_weight[0]
    rows, depth = x.shape
    cols = w.shape[1]
    half = cols // 2
    me = lax.axis_index("mp")
    b = lax.axis_index("batch")
    tower = lax.axis_index("tower")
    nq = 4
    dq = depth // nq
    nt = (((1,), (1,)), ((), ()))
    tn = (((0,), (0,)), ((), ()))

    token = []

    def tie(v, *deps):
        deps = [d for d in (*deps, *token) if d is not None]
        return lax.optimization_barrier((v, *deps))[0] if deps else v

    def wait(v):
        v = tie(v)
        token[:] = [v]
        return v

    def sy(v, *deps):
        return swapped(tie(v, *deps), "mp", 1)

    def sz(v, *deps):
        return swapped(tie(v, *deps), "mp", 2)

    def sp(v, *deps):
        return swapped(tie(v, *deps), "mp", 4)

    def sx(v, *deps):
        return swapped(tie(v, *deps), "batch", 1)

    def st(v, *deps):
        return swapped(tie(v, *deps), "tower", 1)

    def mine(v):
        return lax.dynamic_slice_in_dim(v, b * half, half, v.ndim - 1)

    def other(v):
        return lax.dynamic_slice_in_dim(v, (1 - b) * half, half, v.ndim - 1)

    def natural(m, o):
        return jnp.where(b == 0, jnp.concatenate([m, o], -1), jnp.concatenate([o, m], -1))

    def four(a, c):
        return jnp.concatenate([a[..., :half], c[..., :half], a[..., half:], c[..., half:]], -1)

    def quarter(v, q):
        return v[q * dq : (q + 1) * dq]

    top, low = x[: rows // 2], x[rows // 2 :]
    z1 = sz(top)
    y1 = sy(top)
    w_m = mine(w)
    p = [sp(quarter(w_m, 0)), sp(quarter(w_m, 1)), None, None]

    w_o = other(w)
    coefs = stitch[0]
    self_c = jnp.where(tower == 0, coefs[0], coefs[1])
    other_c = jnp.where(tower == 0, coefs[1], coefs[0])
    small = jnp.stack([self_c, other_c, st(other_c), fc_bias[0].astype(F32)])
    small = jnp.concatenate([mine(small), other(small)], 1)
    grads = image_grad[0]
    grads = jnp.concatenate([mine(grads), other(grads)], 1)

    def square_rows(v):
        v = v.reshape(-1, rows)
        return jnp.concatenate(
            [lax.dynamic_index_in_dim(v, me ^ o, 0, keepdims=False) for o in range(4)], 0
        )

    live = square_rows(row_live).astype(F32)
    img_dev = crop_counts.shape[0]
    local_img = square_rows(row_image) - b * img_dev
    match = local_img[:, None] == jnp.arange(img_dev, dtype=jnp.int32)[None, :]
    per_row = jnp.sum(jnp.where(match, crop_counts[None, :].astype(F32), 0.0), axis=1)
    scale = live / per_row

    def out_grad_of(g):
        picked = jnp.dot(match.astype(BF), g, preferred_element_type=F32)
        return (picked * scale[:, None]).astype(BF)

    og_a = out_grad_of(grads)
    oo_a = st(og_a)
    wa = jnp.concatenate([w_m, w_o], 1)
    pre_a = [jnp.dot(x, wa, preferred_element_type=F32)]

    y1 = wait(y1)
    y2 = sy(low)
    z1 = wait(z1)
    z2 = sz(low)
    x_got = [None] * nq
    p[0] = wait(p[0])
    x_got[0] = sx(p[0])
    p[1] = wait(p[1])
    p[2] = sp(quarter(w_m, 2))
    y2 = wait(y2)
    d1 = sy(z1, pre_a[0])
    x_got[0] = wait(x_got[0])
    x_got[1] = sx(p[1])
    x_y = jnp.concatenate([y1, y2], 0)
    pre_a.append(jnp.dot(x_y, wa, preferred_element_type=F32))
    z2 = wait(z2)
    x_z = jnp.concatenate([z1, z2], 0)
    pre_a.append(jnp.dot(x_z, wa, preferred_element_type=F32))
    p[2] = wait(p[2])
    p[3] = sp(quarter(w_m, 3), pre_a[1])
    x_got[1] = wait(x_got[1])
    x_got[2] = sx(p[2])
    w4 = [None] * nq

    def weights(q):
        return jnp.concatenate(
            [quarter(w_m, q), p[q], quarter(w_o, q), x_got[q]], 1
        )

    def b_cols(q):
        return jnp.concatenate([p[q], x_got[q]], 1)

    def kq(v, q):
        return v[:, q * dq : (q + 1) * dq]

    def dot_b(block, qs, acc):
        for q in qs:
            r = jnp.dot(kq(block, q), b_cols(q), preferred_element_type=F32)
            acc = r if acc is None else acc + r
        return acc

    blocks = [x, x_y, x_z]
    pre_b = [dot_b(v, (0, 1), None) for v in blocks]
    d1 = wait(d1)
    d2 = sy(z2, pre_a[2])
    p[3] = wait(p[3])
    grads_b = sp(grads)
    small_b = sp(small)
    x_got[2] = wait(x_got[2])
    x_got[3] = sx(p[3], *pre_b)
    pre_b = [dot_b(v, (2,), a) for v, a in zip(blocks, pre_b)]
    x_got[3] = wait(x_got[3])
    pre_b = [dot_b(v, (3,), a) for v, a in zip(blocks, pre_b)]
    grads_b = wait(grads_b)
    small_b = wait(small_b)
    og_b = out_grad_of(grads_b)
    oo_b = st(og_b)
    vec = four(small, small_b)
    self4, other4, cross4 = vec[0], vec[1], vec[2]
    out_grad = four(og_a, og_b)
    out_other = four(oo_a, oo_b)
    out_wide = out_grad.astype(F32)
    hidden_grad = (self4[None] * out_wide + cross4[None] * out_other.astype(F32)).astype(BF)

    def activate(a, c, lo):
        pre = four(a + small[3][None], c + small_b[3][None])
        hg = hidden_grad[lo : lo + pre.shape[0]]
        return jnp.maximum(pre, 0.0).astype(BF), jnp.where(pre > 0, hg, jnp.zeros_like(hg))

    hid, pg = [], []
    for o in range(3):
        h, g = activate(pre_a[o], pre_b[o], o * rows)
        hid.append(h)
        pg.append(g)
    w4 = [weights(q) for q in range(nq)]

    def part(o, q):
        return lax.dot_general(pg[o], w4[q], nt, preferred_element_type=F32)

    n_half = rows // 2
    a1 = jnp.dot(d1, wa, preferred_element_type=F32)
    b1 = dot_b(d1, range(nq), None)
    h1, g1 = activate(a1, b1, 3 * rows)
    yd0 = part(1, 0).astype(BF)
    d2 = wait(d2)
    yd = [sy(yd0, g1)] + [None] * 3
    a2 = jnp.dot(d2, wa, preferred_element_type=F32)
    b2 = dot_b(d2, range(nq), None)
    h2, g2 = activate(a2, b2, 3 * rows + n_half)
    hid.append(jnp.concatenate([h1, h2], 0))
    pg.append(jnp.concatenate([g1, g2], 0))
    hidden = jnp.concatenate(hid, 0)
    pre_grad = jnp.concatenate(pg, 0)
    x_all = jnp.concatenate([x, y1, y2, z1, z2, d1, d2], 0)

    def dw_sent(q):
        return lax.dot_general(
            kq(x_all, q), pre_grad[:, cols:], tn, preferred_element_type=F32
        ).astype(BF)

    def dw_kept(q, got):
        r = lax.dot_general(kq(x_all, q), pre_grad[:, :cols], tn, preferred_element_type=F32)
        return r + got.astype(F32)

    s, k, a, t = [None] * nq, [None] * nq, [None] * nq, [None] * nq
    dd, zz = [None] * nq, [None] * nq
    s[0] = sx(dw_sent(0))
    hid_other = st(hidden)
    dq0 = part(3, 0).astype(BF)
    nxt = dw_sent(1)
    yd[0] = wait(yd[0])
    dd[0] = sy(dq0)
    hid_other = wait(hid_other)
    hw, how = hidden.astype(F32), hid_other.astype(F32)
    stitched = ((self4[None] * hw + other4[None] * how) * live[:, None]).astype(BF)
    st_a = jnp.concatenate([stitched[:, :half], stitched[:, cols : cols + half]], 1)
    st_b = jnp.concatenate([stitched[:, half:cols], stitched[:, cols + half :]], 1)
    st_got = sp(st_b)
    dq1 = part(3, 1).astype(BF)
    s[0] = wait(s[0])
    s[1] = sx(nxt)
    kept = dw_kept(0, s[0])
    t[0] = kept[:, :half]
    k[0] = sp(kept[:, half:].astype(BF))
    nxt = dw_sent(2)
    dd[0] = wait(dd[0])
    dd[1] = sy(dq1)
    zz[0] = sz((part(2, 0) + dd[0].astype(F32)).astype(BF))
    dq2 = part(3, 2).astype(BF)
    dd[1] = wait(dd[1])
    dd[2] = sy(dq2)
    st_got = wait(st_got)
    s[1] = wait(s[1])
    s[2] = sx(nxt)
    kept = dw_kept(1, s[1])
    t[1] = kept[:, :half]
    k[0] = wait(k[0])
    k[1] = sp(kept[:, half:].astype(BF))
    zz[0] = wait(zz[0])
    zz[1] = sz((part(2, 1) + dd[1].astype(F32)).astype(BF))
    nxt = dw_sent(3)
    dq3 = part(3, 3).astype(BF)
    dd[2] = wait(dd[2])
    dd[3] = sy(dq3)
    t[0] = t[0] + k[0].astype(F32)
    s[2] = wait(s[2])
    s[3] = sx(nxt)
    kept = dw_kept(2, s[2])
    t[2] = kept[:, :half]
    k[1] = wait(k[1])
    k[2] = sp(kept[:, half:].astype(BF))
    zz[1] = wait(zz[1])
    zz[2] = sz((part(2, 2) + dd[2].astype(F32)).astype(BF))
    yd1 = part(1, 1).astype(BF)
    dd[3] = wait(dd[3])
    yd[1] = sy(yd1)
    t[1] = t[1] + k[1].astype(F32)
    s[3] = wait(s[3])
    a[0] = sx(t[0].astype(BF))
    kept = dw_kept(3, s[3])
    t[3] = kept[:, :half]
    k[2] = wait(k[2])
    k[3] = sp(kept[:, half:].astype(BF))
    zz[2] = wait(zz[2])
    zz[3] = sz((part(2, 3) + dd[3].astype(F32)).astype(BF))
    yd2 = part(1, 2).astype(BF)
    a[0] = wait(a[0])
    a[1] = sx(t[1].astype(BF))
    yd[1] = wait(yd[1])
    yd[2] = sy(yd2)
    t[2] = t[2] + k[2].astype(F32)
    yd3 = part(1, 3).astype(BF)
    a[1] = wait(a[1])
    a[2] = sx(t[2].astype(BF))
    yd[2] = wait(yd[2])
    yd[3] = sy(yd3)
    own = [part(0, q) + yd[q].astype(F32) + zz[q].astype(F32) for q in range(3)]
    outs = [natural(t[q], a[q].astype(F32)) for q in range(2)]
    k[3] = wait(k[3])
    t[3] = t[3] + k[3].astype(F32)
    a[2] = wait(a[2])
    a[3] = sx(t[3].astype(BF))
    outs.append(natural(t[2], a[2].astype(F32)))
    zz[3] = wait(zz[3])
    yd[3] = wait(yd[3])
    own.append(part(0, 3) + yd[3].astype(F32) + zz[3].astype(F32))
    acts_grad = jnp.concatenate([v.astype(BF) for v in own], 1)
    outs.append(natural(t[3], a[3].astype(F32)))
    weight_grad = jnp.concatenate(outs, 0)

    st_all = jnp.concatenate([st_a, st_got], 0)
    st_all = natural(st_all[:, :half], st_all[:, half:])
    st_all = st_all.reshape(8, rows, cols)
    order = jnp.arange(8) ^ me
    stitched_out = st_all[order].reshape(8 * rows, cols)

    sums = jnp.stack(
        [
            jnp.sum(out_wide * hw, axis=0),
            jnp.sum(out_wide * how, axis=0),
            jnp.sum(pre_grad.astype(F32), axis=0),
        ]
    )
    s_a = jnp.concatenate([sums[:, :half], sums[:, cols : cols + half]], 1)
    s_b = jnp.concatenate([sums[:, half:cols], sums[:, cols + half :]], 1)
    s_a = s_a + swapped(s_b, "mp", 4)
    s_a = natural(s_a[:, :half], s_a[:, half:])
    s_a = s_a + swapped(s_a, "batch", 1)
    own_s, other_s = s_a[0], s_a[1]
    stitch_grad = jnp.where(tower == 0, jnp.stack([own_s, other_s]), jnp.stack([other_s, own_s]))
    return (
        stitched_out[None],
        acts_grad[None],
        weight_grad[None],
        s_a[2][None],
        stitch_grad[None],
    )


def solution(mesh):
    placed = (
        P("tower", ("batch", "mp"), None),
        P("tower", None, "mp"),
        P("tower", "mp"),
        P("tower", None, "mp"),
        P("tower", "batch", "mp"),
        P("batch"),
        P("batch"),
        P("batch"),
    )
    per_device = squares if mesh.shape["mp"] == 8 and mesh.shape["batch"] == 2 else general
    return jax.shard_map(
        per_device,
        mesh=mesh,
        in_specs=placed,
        out_specs=(
            P("tower", "batch", "mp"),
            P("tower", ("batch", "mp"), None),
            P("tower", None, "mp"),
            P("tower", "mp"),
            P("tower", None, "mp"),
        ),
        check_vma=False,
    )
```

```python
import functools

import jax
import jax.numpy as jnp
from jax import lax
from jax.experimental import pallas as pl
from jax.experimental.pallas import tpu as pltpu
from jax.sharding import PartitionSpec as P

BF = jnp.bfloat16
F32 = jnp.float32


def swapped(block, axis, mask):
    count = lax.axis_size(axis)
    return lax.ppermute(block, axis, [(i, i ^ mask) for i in range(count)])


def general(acts, fc_weight, fc_bias, stitch, image_grad, crop_counts, row_image, row_live):
    feature_rows = acts[0]
    weight_matrix = fc_weight[0]
    layer_bias = fc_bias[0].astype(jnp.float32)
    coefs = stitch[0]
    grads_img = image_grad[0]
    gathered = lax.all_gather(feature_rows, "mp", axis=0, tiled=True)
    preactivation = (
        jnp.dot(gathered, weight_matrix, preferred_element_type=jnp.float32) + layer_bias[None, :]
    )
    active = preactivation > 0
    hidden = jnp.maximum(preactivation, 0.0).astype(jnp.bfloat16)
    tower = lax.axis_index("tower")
    self_coefficient = jnp.where(tower == 0, coefs[0], coefs[1])
    other_coef = jnp.where(tower == 0, coefs[1], coefs[0])
    partner = swapped(hidden, "tower", 1)
    hidden_wide = hidden.astype(jnp.float32)
    partner_wide = partner.astype(jnp.float32)
    stitched = self_coefficient[None, :] * hidden_wide + other_coef[None, :] * partner_wide
    live = row_live.astype(jnp.float32)
    stitched_out = (stitched * live[:, None]).astype(jnp.bfloat16)
    img_dev = crop_counts.shape[0]
    local_img = row_image - lax.axis_index("batch") * img_dev
    match = local_img[:, None] == jnp.arange(img_dev, dtype=jnp.int32)[None, :]
    per_row = jnp.sum(jnp.where(match, crop_counts[None, :].astype(jnp.float32), 0.0), axis=1)
    row_weighting_scale = live / per_row
    picked = jnp.dot(match.astype(jnp.bfloat16), grads_img, preferred_element_type=jnp.float32)
    out_grad = (picked * row_weighting_scale[:, None]).astype(jnp.bfloat16)
    out_wide = out_grad.astype(jnp.float32)
    returned = swapped(other_coef[None, :] * out_wide, "tower", 1)
    hidden_grad = (self_coefficient[None, :] * out_wide + returned).astype(jnp.bfloat16)
    pre_grad = jnp.where(active, hidden_grad, jnp.zeros_like(hidden_grad))
    own_stitch = jnp.sum(out_wide * hidden_wide, axis=0)
    other_stitch = jnp.sum(out_wide * partner_wide, axis=0)
    stitch_grad = jnp.where(
        tower == 0, jnp.stack([own_stitch, other_stitch]), jnp.stack([other_stitch, own_stitch])
    )
    bias_grad = jnp.sum(pre_grad.astype(jnp.float32), axis=0)
    weight_grad = lax.dot_general(
        gathered, pre_grad, (((0,), (0,)), ((), ())), preferred_element_type=jnp.float32
    )
    weight_grad, bias_grad, stitch_grad = lax.psum((weight_grad, bias_grad, stitch_grad), "batch")
    input_grad = lax.psum_scatter(
        lax.dot_general(
            pre_grad, weight_matrix, (((1,), (1,)), ((), ())), preferred_element_type=jnp.float32
        ),
        "mp",
        scatter_dimension=0,
        tiled=True,
    )
    return (
        stitched_out[None],
        input_grad.astype(jnp.bfloat16)[None],
        weight_grad[None],
        bias_grad[None],
        stitch_grad[None],
    )

STEPS = (
    "+y0", "+z0", "z0", "+z1", "+p0", "+d0", "+o", "+a", "z1", "+z2", "+d1", "p0",
    "+x0", "+p1", "o", "a", "y0", "d0", "x0", "F01", "p1", "+x1", "+p2", "z2",
    "+d2", "p2", "+x2", "+g", "+m", "x1", "F12", "d1", "D02", "x2", "F23", "D23",
    "g", "m", "+b", "d2", "E03", "b", "hg",
)

NT = (((1,), (1,)), ((), ()))
TN = (((0,), (0,)), ((), ()))
LIGHT = pl.CostEstimate(flops=1000, bytes_accessed=1000, transcendentals=0)


def forward_body(n_x, starts, has_acc, *refs):
    xs, rest = refs[:n_x], list(refs[n_x:])
    w_m, w_o = rest.pop(0), rest.pop(0)
    n_q = len(starts) - 1
    ps = [rest.pop(0) for _ in range(n_q)]
    gs = [rest.pop(0) for _ in range(n_q)]
    acc_in = rest.pop(0) if has_acc else None
    out = rest[0]
    i = pl.program_id(0)
    half = w_m.shape[1]

    @pl.when(i == 0)
    def _():
        if has_acc:
            out[...] = acc_in[...]
        else:
            out[...] = jnp.zeros_like(out)

    for q in range(n_q):

        @pl.when((i >= starts[q]) & (i < starts[q + 1]))
        def _():
            lo = 0
            for x in xs:
                rows = x.shape[0]
                for j, w in enumerate((w_m, ps[q], w_o, gs[q])):
                    out[lo : lo + rows, j * half : (j + 1) * half] += jnp.dot(
                        x[...], w[...], preferred_element_type=F32
                    )
                lo += rows


def forward(xs, w_m, w_o, ps, gs, lo, block, acc=None):
    starts = [0]
    for p in ps:
        starts.append(starts[-1] + p.shape[0] // block)
    rows = sum(x.shape[0] for x in xs)
    half = w_m.shape[1]
    operands = [*xs, w_m, w_o, *ps, *gs]
    specs = [pl.BlockSpec((x.shape[0], block), lambda i: (0, lo + i)) for x in xs]
    specs += [pl.BlockSpec((block, half), lambda i: (lo + i, 0))] * 2
    for a, e in [*zip(starts, starts[1:])] * 2:
        specs.append(
            pl.BlockSpec((block, half), lambda i, a=a, e=e: (jnp.clip(i - a, 0, e - a - 1), 0))
        )
    wide = pl.BlockSpec((rows, 4 * half), lambda i: (0, 0))
    if acc is not None:
        operands.append(acc)
        specs.append(wide)
    return pl.pallas_call(
        functools.partial(forward_body, len(xs), starts, acc is not None),
        out_shape=jax.ShapeDtypeStruct((rows, 4 * half), F32),
        grid=(starts[-1],),
        in_specs=specs,
        out_specs=wide,
        cost_estimate=LIGHT,
    )(*operands)


def activate_body(bounds, *refs):
    accs, rest = refs[: len(bounds)], refs[len(bounds) :]
    bias, hg, hid, pre_grad = rest
    i = pl.program_id(0)
    for acc, (lo, hi) in zip(accs, bounds):

        @pl.when((i >= lo) & (i < hi))
        def _():
            pre = acc[...] + bias[...]
            hid[...] = jnp.maximum(pre, 0.0).astype(BF)
            pre_grad[...] = jnp.where(pre > 0, hg[...], jnp.zeros_like(hg))


def activate(accs, bias, hg, rows):
    wide = hg.shape[1]
    bounds, lo = [], 0
    for acc in accs:
        bounds.append((lo, lo + acc.shape[0] // rows))
        lo = bounds[-1][1]
    specs = [
        pl.BlockSpec((rows, wide), lambda i, lo=lo, hi=hi: (jnp.clip(i - lo, 0, hi - lo - 1), 0))
        for lo, hi in bounds
    ]
    at = pl.BlockSpec((rows, wide), lambda i: (i, 0))
    return pl.pallas_call(
        functools.partial(activate_body, bounds),
        out_shape=(jax.ShapeDtypeStruct(hg.shape, BF),) * 2,
        grid=(bounds[-1][1],),
        in_specs=[*specs, pl.BlockSpec((1, wide), lambda i: (0, 0)), at],
        out_specs=[at, at],
        cost_estimate=LIGHT,
    )(*accs, bias, hg)


def nt_body(n_p, n_w, n_add, *refs):
    ps, ws = refs[:n_p], refs[n_p : n_p + n_w]
    adds, out = refs[n_p + n_w : n_p + n_w + n_add], refs[-1]
    weights = jnp.concatenate([w[...] for w in ws], 1)
    rows = ps[0].shape[0]
    for j, p in enumerate(ps):
        r = lax.dot_general(p[...], weights, NT, preferred_element_type=F32)
        for a in adds:
            r = r + a[...].astype(F32)
        out[j * rows : (j + 1) * rows, :] = r.astype(BF)


def nt_product(pre_grad, picks, ws, adds, rows, width, block, into=None):
    steps = width // block
    operands, specs = [], []
    for o in picks:
        operands.append(pre_grad)
        specs.append(pl.BlockSpec((rows, pre_grad.shape[1]), lambda i, o=o: (o, 0)))
    for w, lo in ws:
        operands.append(w)
        specs.append(pl.BlockSpec((block, w.shape[1]), lambda i, lo=lo: (lo + i, 0)))
    for a, r, lo in adds:
        operands.append(a)
        specs.append(pl.BlockSpec((rows, block), lambda i, r=r, lo=lo: (r, lo + i)))
    body = functools.partial(nt_body, len(picks), len(ws), len(adds))
    height = rows * len(picks)
    shape, first, alias = (height, width), 0, {}
    if into is not None:
        held, shape, first = into
        if held is not None:
            alias = {len(operands): 0}
            operands.append(held)
            specs.append(pl.BlockSpec(memory_space=pl.ANY))
            inner = body

            def body(*refs):
                inner(*refs[:-2], refs[-1])

    return pl.pallas_call(
        body,
        out_shape=jax.ShapeDtypeStruct(shape, BF),
        grid=(steps,),
        in_specs=specs,
        out_specs=pl.BlockSpec((height, block), lambda i: (0, first + i)),
        input_output_aliases=alias,
        cost_estimate=LIGHT,
    )(*operands)


def sent_body(n_x, *refs):
    block = jnp.concatenate([x[...] for x in refs[:n_x]], 0)
    p, out = refs[n_x], refs[n_x + 1]
    out[...] = lax.dot_general(block, p[...], TN, preferred_element_type=F32).astype(BF)


def kept_body(n_x, *refs):
    block = jnp.concatenate([x[...] for x in refs[:n_x]], 0)
    p, got, near, far = refs[n_x:]
    r = lax.dot_general(block, p[...], TN, preferred_element_type=F32) + got[...].astype(F32)
    half = near.shape[1]
    near[...] = r[:, :half]
    far[...] = r[:, half:].astype(BF)


def tn_product(xs, pre_grad, side, lo, width, block, got=None):
    cols = pre_grad.shape[1] // 2
    steps = width // block
    operands = [*xs, pre_grad]
    specs = [pl.BlockSpec((x.shape[0], block), lambda i: (0, lo + i)) for x in xs]
    specs.append(pl.BlockSpec((pre_grad.shape[0], cols), lambda i: (0, side)))
    if got is None:
        body = functools.partial(sent_body, len(xs))
        outs = jax.ShapeDtypeStruct((width, cols), BF)
        out_specs = pl.BlockSpec((block, cols), lambda i: (i, 0))
    else:
        body = functools.partial(kept_body, len(xs))
        operands.append(got)
        specs.append(pl.BlockSpec((block, cols), lambda i: (i, 0)))
        half = cols // 2
        outs = (
            jax.ShapeDtypeStruct((width, half), F32),
            jax.ShapeDtypeStruct((width, half), BF),
        )
        out_specs = [pl.BlockSpec((block, half), lambda i: (i, 0))] * 2
    return pl.pallas_call(
        body,
        out_shape=outs,
        grid=(steps,),
        in_specs=specs,
        out_specs=out_specs,
        cost_estimate=LIGHT,
    )(*operands)


def add_body(near, got, out):
    out[...] = (near[...] + got[...].astype(F32)).astype(BF)


def finished(near, got):
    width, half = near.shape
    spec = pl.BlockSpec((width // 2, half), lambda i: (i, 0))
    return pl.pallas_call(
        add_body,
        out_shape=jax.ShapeDtypeStruct((width, half), BF),
        grid=(2,),
        in_specs=[spec, spec],
        out_specs=spec,
        cost_estimate=LIGHT,
    )(near, got)


def place_body(b, near, got, other, *rest):
    out = rest[-1]
    half = near.shape[1]
    total = near[...] + got[...].astype(F32)
    wide = other[...].astype(F32)
    first = b[0] == 0
    out[:, :half] = jnp.where(first, total, wide)
    out[:, half:] = jnp.where(first, wide, total)


def place(b, near, got, other, held, depth, at):
    width, half = near.shape
    spec = pl.BlockSpec((width // 2, half), lambda i, b: (i, 0))
    operands, specs, alias = [near, got, other], [spec] * 3, {}
    if held is not None:
        alias = {4: 0}
        operands.append(held)
        specs.append(pl.BlockSpec(memory_space=pl.ANY))
    return pl.pallas_call(
        place_body,
        out_shape=jax.ShapeDtypeStruct((depth, 2 * half), F32),
        grid_spec=pltpu.PrefetchScalarGridSpec(
            num_scalar_prefetch=1,
            grid=(2,),
            in_specs=specs,
            out_specs=pl.BlockSpec((width // 2, 2 * half), lambda i, b: (2 * at + i, 0)),
        ),
        input_output_aliases=alias,
        cost_estimate=LIGHT,
    )(b, *operands)


def squares(acts, fc_weight, fc_bias, stitch, image_grad, crop_counts, row_image, row_live):
    x = acts[0]
    w = fc_weight[0]
    rows, depth = x.shape
    cols = w.shape[1]
    half = cols // 2
    me = lax.axis_index("mp")
    b = lax.axis_index("batch")
    tower = lax.axis_index("tower")
    nk = 6
    dk = depth // nk
    wat = [0, 3, 5, 6]
    nw = len(wat) - 1
    block = 512 if dk % 512 == 0 else dk

    token = []

    def tie(v, *deps):
        deps = [d for d in (*deps, *token) if d is not None]
        return lax.optimization_barrier((v, *deps))[0] if deps else v

    def wait(v):
        v = tie(v)
        token[:] = [v]
        return v

    def lane(axis, mask):
        return lambda v, *deps: swapped(tie(v, *deps), axis, mask)

    sy = lane("mp", 1)
    sz = lane("mp", 2)
    sp = lane("mp", 4)
    sx = lane("batch", 1)
    st = lane("tower", 1)

    def mine(v):
        return lax.dynamic_slice_in_dim(v, b * half, half, v.ndim - 1)

    def other(v):
        return lax.dynamic_slice_in_dim(v, (1 - b) * half, half, v.ndim - 1)

    def natural(m, o):
        return jnp.where(b == 0, jnp.concatenate([m, o], -1), jnp.concatenate([o, m], -1))

    def four(a, c):
        return jnp.concatenate([a[..., :half], c[..., :half], a[..., half:], c[..., half:]], -1)

    def third(v, q):
        return v[wat[q] * dk : wat[q + 1] * dk]

    w_m = mine(w)
    w_o = other(w)
    coefs = stitch[0]
    self_c = jnp.where(tower == 0, coefs[0], coefs[1])
    other_c = jnp.where(tower == 0, coefs[1], coefs[0])
    grads = image_grad[0]
    grads = jnp.concatenate([mine(grads), other(grads)], 1)

    def square_rows(v):
        v = v.reshape(-1, rows)
        return jnp.concatenate(
            [lax.dynamic_index_in_dim(v, me ^ o, 0, keepdims=False) for o in range(4)], 0
        )

    live = square_rows(row_live).astype(F32)
    img_dev = crop_counts.shape[0]
    local_img = square_rows(row_image) - b * img_dev
    match = local_img[:, None] == jnp.arange(img_dev, dtype=jnp.int32)[None, :]
    per_row = jnp.sum(jnp.where(match, crop_counts[None, :].astype(F32), 0.0), axis=1)
    scale = live / per_row

    def out_grad_of(g):
        picked = jnp.dot(match.astype(BF), g, preferred_element_type=F32)
        return (picked * scale[:, None]).astype(BF)

    nz = 3
    rz = rows // nz
    V = {"X": x, "G": grads, "oc0": other_c}
    for q in range(nw):
        V[f"W{q}"] = third(w_m, q)
    fb = dk
    send = {"z": (sz, "Z"), "y": (sy, "X"), "d": (sy, "z"), "p": (sp, "W"), "x": (sx, "p")}
    once = {"g": (sp, "G"), "m": (sp, "small"), "o": (st, "oc0"), "a": (st, "oga"), "b": (st, "ogb")}

    def known():
        return [x, V["y0"], *(V[f"z{i}"] for i in range(nz - 1))]

    def weight_parts(q0, q1):
        ps = [V[f"p{q}"] for q in range(q0, q1)]
        return ps, [V[f"x{q}"] for q in range(q0, q1)], wat[q0], fb

    for step in STEPS:
        if step[0] == "+":
            key = step[1:]
            if key == "y0":
                V[key] = sy(x)
                continue
            if key in once:
                if key == "m":
                    small = jnp.stack([self_c, other_c, V["o"], fc_bias[0].astype(F32)])
                    V["small"] = jnp.concatenate([mine(small), other(small)], 1)
                elif key == "a":
                    V["oga"] = out_grad_of(grads)
                elif key == "b":
                    V["ogb"] = out_grad_of(V["g"])
                f, src = once[key]
                V[key] = f(V[src])
            else:
                f, src = send[key[0]]
                if src == "Z":
                    i = int(key[1:])
                    V[src + key[1:]] = tie(x)[i * rz : (i + 1) * rz]
                V[key] = f(V[src + key[1:]])
        elif step[0] == "F":
            q0, q1 = int(step[1]), int(step[2])
            xs = known()
            xs[0] = tie(xs[0])
            V["F"] = forward(xs, w_m, w_o, *weight_parts(q0, q1), V.get("F"))
            token[:] = [V["F"]]
        elif step[0] in "DE":
            q0, q1 = int(step[1]), int(step[2])
            rest = [V[f"d{nz - 1}"]]
            if step[0] == "D":
                rest = [V[f"z{nz - 1}"], *(V[f"d{i}"] for i in range(nz - 1))]
            rest[0] = tie(rest[0])
            V[step[0]] = forward(rest, w_m, w_o, *weight_parts(q0, q1), V.get(step[0]))
            token[:] = [V[step[0]]]
        elif step == "hg":
            vec = four(V["small"], V["m"])
            self4, other4, cross4 = vec[0], vec[1], vec[2]
            out_wide = four(V["oga"], V["ogb"]).astype(F32)
            theirs = four(V["a"], V["b"]).astype(F32)
            hidden_grad = (self4[None] * out_wide + cross4[None] * theirs).astype(BF)
            bias4 = vec[3][None]
            V["hg"] = wait(hidden_grad)
        else:
            V[step] = wait(V[step])
    p = [V[f"p{q}"] for q in range(nw)]
    xg = [V[f"x{q}"] for q in range(nw)]
    hidden, pre_grad = activate([V["F"], V["D"], V["E"]], bias4, V["hg"], rz)
    features = [*known(), V[f"z{nz - 1}"], *(V[f"d{i}"] for i in range(nz))]
    per = dk // block

    def weights(c):
        q = max(i for i in range(nw) if wat[i] <= c)
        lo = (c - wat[q]) * per
        return [(w_m, c * per), (p[q], lo), (w_o, c * per), (xg[q], lo)]

    def only(v, *deps):
        return lax.optimization_barrier((v, *deps))[0] if deps else v

    def y_part(c, *deps):
        return nt_product(only(pre_grad, *deps), (1, 3), weights(c), (), rows, dk, block)

    def z_part(c, *deps):
        g = only(pre_grad, *deps)
        return nt_product(g, (2,), weights(c), [(yy[c], 1, 0)], rows, dk, block)

    def own_part(c, held):
        into = (held, (rows, depth), c * per)
        return nt_product(
            pre_grad, (0,), weights(c), [(yy[c], 0, 0), (zz[c], 0, 0)], rows, dk, block, into
        )

    def dw_sent(c, *deps):
        return tn_product(features, only(pre_grad, *deps), 1, c * per, dk, block)

    def dw_kept(c):
        return tn_product(features, pre_grad, 0, c * per, dk, block, s[c])

    token.clear()
    bvec = jnp.full((1,), b, jnp.int32)

    s, k, a, t, k_got = ([None] * nk for _ in range(5))
    yy, zz, own, put = ([None] * nk for _ in range(4))

    hid_other = None
    later = {}

    def do_sums():
        hw, how = hidden.astype(F32), hid_other.astype(F32)
        sums = jnp.stack(
            [
                jnp.sum(out_wide * hw, axis=0),
                jnp.sum(out_wide * how, axis=0),
                jnp.sum(pre_grad.astype(F32), axis=0),
            ]
        )
        later["a"] = jnp.concatenate([sums[:, :half], sums[:, cols : cols + half]], 1)
        s_b = jnp.concatenate([sums[:, half:cols], sums[:, cols + half :]], 1)
        later["p"] = sp(s_b)

    def do_st():
        hw, how = hidden.astype(F32), hid_other.astype(F32)
        stitched = ((self4[None] * hw + other4[None] * how) * live[:, None]).astype(BF)
        later["st_a"] = jnp.concatenate([stitched[:, :half], stitched[:, cols : cols + half]], 1)
        st_b = jnp.concatenate([stitched[:, half:cols], stitched[:, cols + half :]], 1)
        later["st"] = sp(st_b)

    def do_sumx():
        s_a = later["a"] + later["p"]
        s_a = natural(s_a[:, :half], s_a[:, half:])
        later["s"] = s_a + sx(s_a)

    def lump(n, *extra):
        places = [(v, c) for v, c in ((yy, n), (s, n), (zz, n - 1), (k_got, n - 1), (a, n - 2))
                  if 0 <= c < nk and v[c] is not None]
        outs = lax.optimization_barrier((*(v[c] for v, c in places), *extra))
        for (v, c), o in zip(places, outs):
            v[c] = o
        held = [v[c] for v, c in ((own, n - 2), (put, n - 3)) if 0 <= c < nk]
        token[:] = [*outs, *held]
        return outs[len(places):]

    def st_piece(half_rows):
        lo, hi = half_rows
        hw, how = hidden[lo:hi].astype(F32), hid_other[lo:hi].astype(F32)
        stitched = (self4[None] * hw + other4[None] * how) * live[lo:hi, None]
        stitched = stitched.astype(BF)
        kept = jnp.concatenate([stitched[:, :half], stitched[:, cols : cols + half]], 1)
        sent = jnp.concatenate([stitched[:, half:cols], stitched[:, cols + half :]], 1)
        return kept, sp(sent)

    y_next, s_next = y_part(0), None
    cut = 960 * rows // 384
    for n in range(nk + 2):
        if n < nk:
            yy[n] = sy(y_next, s_next)
            if n == 0:
                s_next = dw_sent(0, y_next)
            s[n] = sx(s_next)
        extra = []
        if n == 0:
            hid_other = st(only(hidden, y_next))
            do_sums()
            st_a0, st_g0 = st_piece((0, cut))
            extra = [later["p"], st_g0]
        if 0 < n <= nk:
            zz[n - 1] = sz(z_part(n - 1))
            t[n - 1], k[n - 1] = dw_kept(n - 1)
            k_got[n - 1] = sp(k[n - 1])
        if n == nk + 1 and cut < 4 * rows:
            st_a1, st_g1 = st_piece((cut, 4 * rows))
        if n == 1:
            do_sumx()
            extra = [later["s"]]
        if 1 < n:
            a[n - 2] = sx(finished(t[n - 2], k_got[n - 2]))
            own[n - 2] = own_part(n - 2, own[n - 3] if n > 2 else None)
        if 2 < n:
            put[n - 3] = place(
                bvec, t[n - 3], k_got[n - 3], a[n - 3], put[n - 4] if n > 3 else None, depth, n - 3
            )
        if n + 1 < nk:
            y_next, s_next = y_part(n + 1), dw_sent(n + 1)
        outs = lump(n, *extra)
        if n == 0:
            later["p"], st_g0 = outs
        if n == 1:
            (later["s"],) = outs
    token.clear()
    put[-1] = place(bvec, t[-1], k_got[-1], a[-1], put[-2], depth, nk - 1)
    later["st_a"], later["st"] = st_a0, st_g0
    if cut < 4 * rows:
        later["st_a"] = jnp.concatenate([st_a0, st_a1], 0)
        later["st"] = jnp.concatenate([st_g0, st_g1], 0)
    held_x, held_w = own[-1], put[-1]
    st_a, st_got, s_a = later["st_a"], later["st"], later["s"]
    acts_grad, weight_grad = held_x, held_w

    st_all = jnp.concatenate([st_a, st_got], 0)
    st_all = natural(st_all[:, :half], st_all[:, half:])
    st_all = st_all.reshape(8, rows, cols)
    order = jnp.arange(8) ^ me
    stitched_out = st_all[order].reshape(8 * rows, cols)

    own_s, other_s = s_a[0], s_a[1]
    stitch_grad = jnp.where(tower == 0, jnp.stack([own_s, other_s]), jnp.stack([other_s, own_s]))
    return (
        stitched_out[None],
        acts_grad[None],
        weight_grad[None],
        s_a[2][None],
        stitch_grad[None],
    )


def solution(mesh):
    placed = (
        P("tower", ("batch", "mp"), None),
        P("tower", None, "mp"),
        P("tower", "mp"),
        P("tower", None, "mp"),
        P("tower", "batch", "mp"),
        P("batch"),
        P("batch"),
        P("batch"),
    )
    per_device = squares if mesh.shape["mp"] == 8 and mesh.shape["batch"] == 2 else general
    return jax.shard_map(
        per_device,
        mesh=mesh,
        in_specs=placed,
        out_specs=(
            P("tower", "batch", "mp"),
            P("tower", ("batch", "mp"), None),
            P("tower", None, "mp"),
            P("tower", "mp"),
            P("tower", None, "mp"),
        ),
        check_vma=False,
    )
```

```python
import functools

import jax
import jax.numpy as jnp
from jax import lax
from jax.experimental import pallas as pl
from jax.experimental.pallas import tpu as pltpu
from jax.sharding import PartitionSpec as P

BF = jnp.bfloat16
F32 = jnp.float32


def swapped(block, axis, mask):
    count = lax.axis_size(axis)
    return lax.ppermute(block, axis, [(i, i ^ mask) for i in range(count)])


def general(acts, fc_weight, fc_bias, stitch, image_grad, crop_counts, row_image, row_live):
    feature_rows = acts[0]
    weight_matrix = fc_weight[0]
    layer_bias = fc_bias[0].astype(jnp.float32)
    coefs = stitch[0]
    grads_img = image_grad[0]
    gathered = lax.all_gather(feature_rows, "mp", axis=0, tiled=True)
    preactivation = (
        jnp.dot(gathered, weight_matrix, preferred_element_type=jnp.float32) + layer_bias[None, :]
    )
    active = preactivation > 0
    hidden = jnp.maximum(preactivation, 0.0).astype(jnp.bfloat16)
    tower = lax.axis_index("tower")
    self_coefficient = jnp.where(tower == 0, coefs[0], coefs[1])
    other_coef = jnp.where(tower == 0, coefs[1], coefs[0])
    partner = swapped(hidden, "tower", 1)
    hidden_wide = hidden.astype(jnp.float32)
    partner_wide = partner.astype(jnp.float32)
    stitched = self_coefficient[None, :] * hidden_wide + other_coef[None, :] * partner_wide
    live = row_live.astype(jnp.float32)
    stitched_out = (stitched * live[:, None]).astype(jnp.bfloat16)
    img_dev = crop_counts.shape[0]
    local_img = row_image - lax.axis_index("batch") * img_dev
    match = local_img[:, None] == jnp.arange(img_dev, dtype=jnp.int32)[None, :]
    per_row = jnp.sum(jnp.where(match, crop_counts[None, :].astype(jnp.float32), 0.0), axis=1)
    row_weighting_scale = live / per_row
    picked = jnp.dot(match.astype(jnp.bfloat16), grads_img, preferred_element_type=jnp.float32)
    out_grad = (picked * row_weighting_scale[:, None]).astype(jnp.bfloat16)
    out_wide = out_grad.astype(jnp.float32)
    returned = swapped(other_coef[None, :] * out_wide, "tower", 1)
    hidden_grad = (self_coefficient[None, :] * out_wide + returned).astype(jnp.bfloat16)
    pre_grad = jnp.where(active, hidden_grad, jnp.zeros_like(hidden_grad))
    own_stitch = jnp.sum(out_wide * hidden_wide, axis=0)
    other_stitch = jnp.sum(out_wide * partner_wide, axis=0)
    stitch_grad = jnp.where(
        tower == 0, jnp.stack([own_stitch, other_stitch]), jnp.stack([other_stitch, own_stitch])
    )
    bias_grad = jnp.sum(pre_grad.astype(jnp.float32), axis=0)
    weight_grad = lax.dot_general(
        gathered, pre_grad, (((0,), (0,)), ((), ())), preferred_element_type=jnp.float32
    )
    weight_grad, bias_grad, stitch_grad = lax.psum((weight_grad, bias_grad, stitch_grad), "batch")
    input_grad = lax.psum_scatter(
        lax.dot_general(
            pre_grad, weight_matrix, (((1,), (1,)), ((), ())), preferred_element_type=jnp.float32
        ),
        "mp",
        scatter_dimension=0,
        tiled=True,
    )
    return (
        stitched_out[None],
        input_grad.astype(jnp.bfloat16)[None],
        weight_grad[None],
        bias_grad[None],
        stitch_grad[None],
    )

STEPS = (
    "+y0", "+z0", "+o", "o", "z0", "+z1", "+p0", "+d0", "+a", "z1", "+z2", "+d1",
    "p0", "+x0", "+p1", "a", "y0", "d0", "x0", "F01", "p1", "+x1", "+p2", "z2",
    "+d2", "p2", "+x2", "+g", "+m", "x1", "d1", "D02", "x2", "F13", "D23", "d2",
    "g", "m", "+b", "E03", "b",
)

NT = (((1,), (1,)), ((), ()))
TN = (((0,), (0,)), ((), ()))
HEAVY = pl.CostEstimate(flops=1000, bytes_accessed=60000000, transcendentals=0)
LIGHT = pl.CostEstimate(flops=1000, bytes_accessed=1000, transcendentals=0)


def forward_body(n_x, starts, has_acc, *refs):
    xs, rest = refs[:n_x], list(refs[n_x:])
    w_m, w_o = rest.pop(0), rest.pop(0)
    n_q = len(starts) - 1
    ps = [rest.pop(0) for _ in range(n_q)]
    gs = [rest.pop(0) for _ in range(n_q)]
    acc_in = rest.pop(0) if has_acc else None
    out = rest[0]
    i = pl.program_id(0)
    half = w_m.shape[1]

    @pl.when(i == 0)
    def _():
        if has_acc:
            out[...] = acc_in[...]
        else:
            out[...] = jnp.zeros_like(out)

    for q in range(n_q):

        @pl.when((i >= starts[q]) & (i < starts[q + 1]))
        def _():
            lo = 0
            for x in xs:
                rows = x.shape[0]
                for j, w in enumerate((w_m, ps[q], w_o, gs[q])):
                    out[lo : lo + rows, j * half : (j + 1) * half] += jnp.dot(
                        x[...], w[...], preferred_element_type=F32
                    )
                lo += rows


def forward(xs, w_m, w_o, ps, gs, lo, block, acc=None):
    starts = [0]
    for p in ps:
        starts.append(starts[-1] + p.shape[0] // block)
    rows = sum(x.shape[0] for x in xs)
    half = w_m.shape[1]
    operands = [*xs, w_m, w_o, *ps, *gs]
    specs = [pl.BlockSpec((x.shape[0], block), lambda i: (0, lo + i)) for x in xs]
    specs += [pl.BlockSpec((block, half), lambda i: (lo + i, 0))] * 2
    for a, e in [*zip(starts, starts[1:])] * 2:
        specs.append(
            pl.BlockSpec((block, half), lambda i, a=a, e=e: (jnp.clip(i - a, 0, e - a - 1), 0))
        )
    wide = pl.BlockSpec((rows, 4 * half), lambda i: (0, 0))
    if acc is not None:
        operands.append(acc)
        specs.append(wide)
    return pl.pallas_call(
        functools.partial(forward_body, len(xs), starts, acc is not None),
        out_shape=jax.ShapeDtypeStruct((rows, 4 * half), F32),
        grid=(starts[-1],),
        in_specs=specs,
        out_specs=wide,
        cost_estimate=LIGHT,
    )(*operands)


def activate_body(bounds, *refs):
    accs, (vec, og_a, og_b, oo_a, oo_b, hid, pre_grad) = refs[: len(bounds)], refs[len(bounds) :]
    i = pl.program_id(0)
    half = og_a.shape[1] // 2
    for acc, (lo, hi) in zip(accs, bounds):

        @pl.when((i >= lo) & (i < hi))
        def _():
            for j in range(4):
                at = slice(j * half, (j + 1) * half)
                part = slice(j // 2 * half, (j // 2 + 1) * half)
                og, oo = (og_b, oo_b) if j % 2 else (og_a, oo_a)
                pre = acc[:, at] + vec[3:4, at]
                hg = vec[0:1, at] * og[:, part].astype(F32) + vec[2:3, at] * oo[:, part].astype(F32)
                hid[:, at] = jnp.maximum(pre, 0.0).astype(BF)
                pre_grad[:, at] = jnp.where(pre > 0, hg.astype(BF), jnp.zeros(hg.shape, BF))


def activate(accs, vec, ogs, rows):
    wide = vec.shape[1]
    total = ogs[0].shape[0]
    bounds, lo = [], 0
    for acc in accs:
        bounds.append((lo, lo + acc.shape[0] // rows))
        lo = bounds[-1][1]
    specs = [
        pl.BlockSpec((rows, wide), lambda i, lo=lo, hi=hi: (jnp.clip(i - lo, 0, hi - lo - 1), 0))
        for lo, hi in bounds
    ]
    specs.append(pl.BlockSpec(vec.shape, lambda i: (0, 0)))
    specs += [pl.BlockSpec((rows, wide // 2), lambda i: (i, 0))] * 4
    at = pl.BlockSpec((rows, wide), lambda i: (i, 0))
    return pl.pallas_call(
        functools.partial(activate_body, bounds),
        out_shape=(jax.ShapeDtypeStruct((total, wide), BF),) * 2,
        grid=(bounds[-1][1],),
        in_specs=specs,
        out_specs=[at, at],
        cost_estimate=LIGHT,
    )(*accs, vec, *ogs)


def nt_body(n_p, n_w, n_add, *refs):
    ps, ws = refs[:n_p], refs[n_p : n_p + n_w]
    adds, out = refs[n_p + n_w : n_p + n_w + n_add], refs[-1]
    weights = jnp.concatenate([w[...] for w in ws], 1)
    rows = ps[0].shape[0]
    for j, p in enumerate(ps):
        r = lax.dot_general(p[...], weights, NT, preferred_element_type=F32)
        for a in adds:
            r = r + a[...].astype(F32)
        out[j * rows : (j + 1) * rows, :] = r.astype(BF)


def nt_product(pre_grad, picks, ws, adds, rows, width, block, into=None, cost=LIGHT):
    steps = width // block
    operands, specs = [], []
    for o in picks:
        operands.append(pre_grad)
        specs.append(pl.BlockSpec((rows, pre_grad.shape[1]), lambda i, o=o: (o, 0)))
    for w, lo in ws:
        operands.append(w)
        specs.append(pl.BlockSpec((block, w.shape[1]), lambda i, lo=lo: (lo + i, 0)))
    for a, r, lo in adds:
        operands.append(a)
        specs.append(pl.BlockSpec((rows, block), lambda i, r=r, lo=lo: (r, lo + i)))
    body = functools.partial(nt_body, len(picks), len(ws), len(adds))
    height = rows * len(picks)
    shape, first, alias = (height, width), 0, {}
    if into is not None:
        held, shape, first = into
        if held is not None:
            alias = {len(operands): 0}
            operands.append(held)
            specs.append(pl.BlockSpec(memory_space=pl.ANY))
            inner = body

            def body(*refs):
                inner(*refs[:-2], refs[-1])

    return pl.pallas_call(
        body,
        out_shape=jax.ShapeDtypeStruct(shape, BF),
        grid=(steps,),
        in_specs=specs,
        out_specs=pl.BlockSpec((height, block), lambda i: (0, first + i)),
        input_output_aliases=alias,
        cost_estimate=cost,
    )(*operands)


def sent_body(n_x, *refs):
    block = jnp.concatenate([x[...] for x in refs[:n_x]], 0)
    p, out = refs[n_x], refs[n_x + 1]
    out[...] = lax.dot_general(block, p[...], TN, preferred_element_type=F32).astype(BF)


def kept_body(n_x, *refs):
    block = jnp.concatenate([x[...] for x in refs[:n_x]], 0)
    p, got, near, far = refs[n_x:]
    r = lax.dot_general(block, p[...], TN, preferred_element_type=F32) + got[...].astype(F32)
    half = near.shape[1]
    near[...] = r[:, :half]
    far[...] = r[:, half:].astype(BF)


def tn_product(xs, pre_grad, side, lo, width, block, got=None):
    cols = pre_grad.shape[1] // 2
    steps = width // block
    operands = [*xs, pre_grad]
    specs = [pl.BlockSpec((x.shape[0], block), lambda i: (0, lo + i)) for x in xs]
    specs.append(pl.BlockSpec((pre_grad.shape[0], cols), lambda i: (0, side)))
    if got is None:
        body = functools.partial(sent_body, len(xs))
        outs = jax.ShapeDtypeStruct((width, cols), BF)
        out_specs = pl.BlockSpec((block, cols), lambda i: (i, 0))
    else:
        body = functools.partial(kept_body, len(xs))
        operands.append(got)
        specs.append(pl.BlockSpec((block, cols), lambda i: (i, 0)))
        half = cols // 2
        outs = (
            jax.ShapeDtypeStruct((width, half), F32),
            jax.ShapeDtypeStruct((width, half), BF),
        )
        out_specs = [pl.BlockSpec((block, half), lambda i: (i, 0))] * 2
    return pl.pallas_call(
        body,
        out_shape=outs,
        grid=(steps,),
        in_specs=specs,
        out_specs=out_specs,
        cost_estimate=LIGHT,
    )(*operands)


def add_body(near, got, out):
    out[...] = (near[...] + got[...].astype(F32)).astype(BF)


def finished(near, got):
    width, half = near.shape
    spec = pl.BlockSpec((width // 2, half), lambda i: (i, 0))
    return pl.pallas_call(
        add_body,
        out_shape=jax.ShapeDtypeStruct((width, half), BF),
        grid=(2,),
        in_specs=[spec, spec],
        out_specs=spec,
        cost_estimate=LIGHT,
    )(near, got)


def place_body(b, near, got, other, *rest):
    out = rest[-1]
    half = near.shape[1]
    total = near[...] + got[...].astype(F32)
    wide = other[...].astype(F32)
    first = b[0] == 0
    out[:, :half] = jnp.where(first, total, wide)
    out[:, half:] = jnp.where(first, wide, total)


def place(b, near, got, other, held, depth, at, cost=LIGHT):
    width, half = near.shape
    spec = pl.BlockSpec((width // 2, half), lambda i, b: (i, 0))
    operands, specs, alias = [near, got, other], [spec] * 3, {}
    if held is not None:
        alias = {4: 0}
        operands.append(held)
        specs.append(pl.BlockSpec(memory_space=pl.ANY))
    return pl.pallas_call(
        place_body,
        out_shape=jax.ShapeDtypeStruct((depth, 2 * half), F32),
        grid_spec=pltpu.PrefetchScalarGridSpec(
            num_scalar_prefetch=1,
            grid=(2,),
            in_specs=specs,
            out_specs=pl.BlockSpec((width // 2, 2 * half), lambda i, b: (2 * at + i, 0)),
        ),
        input_output_aliases=alias,
        cost_estimate=cost,
    )(b, *operands)


def lay(where, pieces, held, height, rows):
    width = pieces[0].shape[1]
    operands, specs, bounds, lo = [], [], [], 0
    for v in pieces:
        n = v.shape[0] // rows
        operands.append(v)
        specs.append(
            pl.BlockSpec((rows, width), lambda i, at, lo=lo, n=n: (jnp.clip(i - lo, 0, n - 1), 0))
        )
        bounds.append((lo, lo + n))
        lo += n
    alias = {}
    if held is not None:
        alias = {len(operands) + 1: 0}
        operands.append(held)
        specs.append(pl.BlockSpec(memory_space=pl.ANY))

    def body(at, *refs):
        out = refs[-1]
        half = width // 2
        i = pl.program_id(0)
        for ref, (a, e) in zip(refs, bounds):

            @pl.when((i >= a) & (i < e))
            def _():
                m, o = ref[:, :half].astype(F32), ref[:, half:].astype(F32)
                first = at[0] == 0
                out[:, :half] = jnp.where(first, m, o).astype(BF)
                out[:, half:] = jnp.where(first, o, m).astype(BF)

    return pl.pallas_call(
        body,
        out_shape=jax.ShapeDtypeStruct((height, width), BF),
        grid_spec=pltpu.PrefetchScalarGridSpec(
            num_scalar_prefetch=1,
            grid=(lo,),
            in_specs=specs,
            out_specs=pl.BlockSpec((rows, width), lambda i, at: (at[i + 1], 0)),
        ),
        input_output_aliases=alias,
        cost_estimate=HEAVY,
    )(where, *operands)


def squares(acts, fc_weight, fc_bias, stitch, image_grad, crop_counts, row_image, row_live):
    x = acts[0]
    w = fc_weight[0]
    rows, depth = x.shape
    cols = w.shape[1]
    half = cols // 2
    me = lax.axis_index("mp")
    b = lax.axis_index("batch")
    tower = lax.axis_index("tower")
    nk = 6
    dk = depth // nk
    wat = (0, 3, 5, 6)
    nw = len(wat) - 1
    block = 512 if dk % 512 == 0 else dk

    token = []

    def tie(v, *deps):
        deps = [d for d in (*deps, *token) if d is not None]
        return lax.optimization_barrier((v, *deps))[0] if deps else v

    def only(v, *deps):
        return lax.optimization_barrier((v, *deps))[0] if deps else v

    def wait(v):
        v = tie(v)
        token[:] = [v]
        return v

    def lane(axis, mask):
        return lambda v, *deps: swapped(tie(v, *deps), axis, mask)

    sy = lane("mp", 1)
    sz = lane("mp", 2)
    sp = lane("mp", 4)
    sx = lane("batch", 1)
    st = lane("tower", 1)

    def mine(v):
        return lax.dynamic_slice_in_dim(v, b * half, half, v.ndim - 1)

    def other(v):
        return lax.dynamic_slice_in_dim(v, (1 - b) * half, half, v.ndim - 1)

    def natural(m, o):
        return jnp.where(b == 0, jnp.concatenate([m, o], -1), jnp.concatenate([o, m], -1))

    def four(a, c):
        return jnp.concatenate([a[..., :half], c[..., :half], a[..., half:], c[..., half:]], -1)

    def third(v, q):
        return v[wat[q] * dk : wat[q + 1] * dk]

    w_m = mine(w)
    w_o = other(w)
    coefs = stitch[0]
    self_c = jnp.where(tower == 0, coefs[0], coefs[1])
    other_c = jnp.where(tower == 0, coefs[1], coefs[0])
    grads = image_grad[0]
    grads = jnp.concatenate([mine(grads), other(grads)], 1)

    def square_rows(v):
        v = v.reshape(-1, rows)
        return jnp.concatenate(
            [lax.dynamic_index_in_dim(v, me ^ o, 0, keepdims=False) for o in range(4)], 0
        )

    live = square_rows(row_live).astype(F32)
    img_dev = crop_counts.shape[0]
    local_img = square_rows(row_image) - b * img_dev
    match = local_img[:, None] == jnp.arange(img_dev, dtype=jnp.int32)[None, :]
    per_row = jnp.sum(jnp.where(match, crop_counts[None, :].astype(F32), 0.0), axis=1)
    scale = live / per_row

    def out_grad_of(g):
        picked = jnp.dot(match.astype(BF), g, preferred_element_type=F32)
        return (picked * scale[:, None]).astype(BF)

    zat = [c * rows // 384 for c in (0, 128, 256, 384)]
    nz = len(zat) - 1
    rz = rows - zat[-2]
    first = x[: zat[1]]
    late = lax.optimization_barrier((x, first))[0]
    V = {"X": x, "G": grads, "oc0": other_c}
    for i in range(nz):
        V[f"Z{i}"] = first if i == 0 else late[zat[i] : zat[i + 1]]
    for q in range(nw):
        V[f"W{q}"] = third(w_m, q)
    fb = dk
    send = {"z": (sz, "Z"), "y": (sy, "X"), "d": (sy, "z"), "p": (sp, "W"), "x": (sx, "p")}
    once = {"g": (sp, "G"), "m": (sp, "small"), "o": (st, "oc0"), "a": (st, "oga"), "b": (st, "ogb")}

    def known():
        return [x, V["y0"], *(V[f"z{i}"] for i in range(nz - 1))]

    def weight_parts(q0, q1):
        ps = [V[f"p{q}"] for q in range(q0, q1)]
        return ps, [V[f"x{q}"] for q in range(q0, q1)], wat[q0], fb

    for step in STEPS:
        if step[0] == "+":
            key = step[1:]
            if key == "y0":
                V[key] = sy(x)
                continue
            if key in once:
                if key == "o":
                    names = [n for n in V if n[0] in "ZW" and n != "Z0"]
                    cut = lax.optimization_barrier((other_c, *(V[n] for n in names)))
                    V.update(zip(["oc0", *names], cut))
                elif key == "m":
                    small = jnp.stack([self_c, other_c, V["o"], fc_bias[0].astype(F32)])
                    V["small"] = jnp.concatenate([mine(small), other(small)], 1)
                elif key == "a":
                    V["oga"] = out_grad_of(grads)
                elif key == "b":
                    V["ogb"] = out_grad_of(V["g"])
                f, src = once[key]
                V[key] = f(V[src])
            else:
                f, src = send[key[0]]
                V[key] = f(V[src + key[1:]])
        elif step[0] == "F":
            q0, q1 = int(step[1]), int(step[2])
            xs = known()
            xs[0] = tie(xs[0])
            V["F"] = forward(xs, w_m, w_o, *weight_parts(q0, q1), V.get("F"))
            token[:] = [V["F"]]
        elif step[0] in "DE":
            q0, q1 = int(step[1]), int(step[2])
            rest = [V[f"d{nz - 1}"]]
            if step[0] == "D":
                rest = [V[f"z{nz - 1}"], *(V[f"d{i}"] for i in range(nz - 1))]
            rest[0] = tie(rest[0])
            V[step[0]] = forward(rest, w_m, w_o, *weight_parts(q0, q1), V.get(step[0]))
            token[:] = [V[step[0]]]
        else:
            V[step] = wait(V[step])
    p = [V[f"p{q}"] for q in range(nw)]
    xg = [V[f"x{q}"] for q in range(nw)]
    vec = four(V["small"], V["m"])
    self4, other4 = vec[0], vec[1]
    ogs = [V[n] for n in ("oga", "ogb", "a", "b")]
    hidden, pre_grad = activate([V["F"], V["D"], V["E"]], vec, ogs, rz)
    features = [*known(), V[f"z{nz - 1}"], *(V[f"d{i}"] for i in range(nz))]
    per = dk // block

    def weights(c):
        q = max(i for i in range(nw) if wat[i] <= c)
        lo = (c - wat[q]) * per
        return [(w_m, c * per), (p[q], lo), (w_o, c * per), (xg[q], lo)]

    def y_part(c, *deps):
        return nt_product(only(pre_grad, *deps), (1, 3), weights(c), (), rows, dk, block)

    def z_part(c, *deps):
        g = only(pre_grad, *deps)
        return nt_product(g, (2,), weights(c), [(yy[c], 1, 0)], rows, dk, block)

    def own_part(c, held, *deps):
        into = (held, (rows, depth), c * per)
        g = only(pre_grad, *deps)
        return nt_product(
            g, (0,), weights(c), [(yy[c], 0, 0), (zz[c], 0, 0)], rows, dk, block, into,
            HEAVY if c == nk - 1 else LIGHT,
        )

    def dw_sent(c, *deps):
        return tn_product(features, only(pre_grad, *deps), 1, c * per, dk, block)

    def dw_kept(c):
        return tn_product(features, pre_grad, 0, c * per, dk, block, s[c])

    token.clear()
    bvec = jnp.full((1,), b, jnp.int32)

    s, k, a, t, k_got = ([None] * nk for _ in range(5))
    yy, zz, own, put = ([None] * nk for _ in range(4))

    hid_other = None
    later = {}

    def do_sums():
        hw, how = hidden.astype(F32), hid_other.astype(F32)
        sums = jnp.stack(
            [
                jnp.sum(out_wide * hw, axis=0),
                jnp.sum(out_wide * how, axis=0),
                jnp.sum(pre_grad.astype(F32), axis=0),
            ]
        )
        later["a"] = jnp.concatenate([sums[:, :half], sums[:, cols : cols + half]], 1)
        s_b = jnp.concatenate([sums[:, half:cols], sums[:, cols + half :]], 1)
        later["p"] = sp(s_b)

    def do_st():
        hw, how = hidden.astype(F32), hid_other.astype(F32)
        stitched = ((self4[None] * hw + other4[None] * how) * live[:, None]).astype(BF)
        later["st_a"] = jnp.concatenate([stitched[:, :half], stitched[:, cols : cols + half]], 1)
        st_b = jnp.concatenate([stitched[:, half:cols], stitched[:, cols + half :]], 1)
        later["st"] = sp(st_b)

    def do_sumx():
        s_a = later["a"] + later["p"]
        s_a = natural(s_a[:, :half], s_a[:, half:])
        later["s"] = s_a + sx(s_a)

    def lump(n, *extra):
        places = [(v, c) for v, c in ((yy, n), (s, n), (zz, n - 1), (k_got, n - 1), (a, n - 2))
                  if 0 <= c < nk and v[c] is not None]
        outs = lax.optimization_barrier((*(v[c] for v, c in places), *extra))
        for (v, c), o in zip(places, outs):
            v[c] = o
        held = [v[c] for v, c in ((own, n - 2), (put, n - 3)) if 0 <= c < nk]
        token[:] = [*outs, *held]
        return outs[len(places):]

    def st_piece(half_rows):
        lo, hi = half_rows
        hw, how = hidden[lo:hi].astype(F32), hid_other[lo:hi].astype(F32)
        stitched = (self4[None] * hw + other4[None] * how) * live[lo:hi, None]
        stitched = stitched.astype(BF)
        kept = jnp.concatenate([stitched[:, :half], stitched[:, cols : cols + half]], 1)
        sent = jnp.concatenate([stitched[:, half:cols], stitched[:, cols + half :]], 1)
        return kept, sp(sent)

    y_next, s_next = y_part(0), None
    cuts = [c * rows // 384 for c in (0, 960, 1536)]
    st_kept, st_got = [], []
    for n in range(nk + 2):
        if n < nk:
            yy[n] = sy(y_next, s_next)
            if n == 0:
                s_next = dw_sent(0, y_next)
            s[n] = sx(s_next)
        extra = []
        if n == 0:
            hid_other = st(only(hidden, y_next))
            out_wide = four(only(V["oga"], s_next), V["ogb"]).astype(F32)
            do_sums()
        if n in (0, 7):
            piece = (0, 7).index(n)
            kept, got_st = st_piece((cuts[piece], cuts[piece + 1]))
            st_kept.append(kept)
            if n == nk + 1:
                st_got.append(got_st)
            else:
                extra.append(got_st)
        if 0 < n <= nk:
            zz[n - 1] = sz(z_part(n - 1))
            t[n - 1], k[n - 1] = dw_kept(n - 1)
            k_got[n - 1] = sp(k[n - 1])
        if n == 0:
            extra = [later["p"], *extra]
        if n == 1:
            do_sumx()
            extra = [later["s"]]
        if 1 < n:
            a[n - 2] = sx(finished(t[n - 2], k_got[n - 2]))
            own[n - 2] = own_part(n - 2, own[n - 3] if n > 2 else None)
        if 2 < n:
            put[n - 3] = place(
                bvec, t[n - 3], k_got[n - 3], a[n - 3], put[n - 4] if n > 3 else None, depth, n - 3,
                HEAVY if n == nk + 1 else LIGHT,
            )
        if n + 1 < nk:
            y_next, s_next = y_part(n + 1), dw_sent(n + 1)
        outs = lump(n, *extra)
        if n == 0:
            later["p"], *outs = outs
        if n == 1:
            later["s"], *outs = outs
        st_got += outs
    token.clear()
    put[-1] = place(bvec, t[-1], k_got[-1], a[-1], put[-2], depth, nk - 1)
    held_x, held_w = own[-1], put[-1]
    s_a = later["s"]
    acts_grad, weight_grad = held_x, held_w

    piece = rows // 2
    tops = [lo // piece for lo in cuts]
    spots = [2 * (me ^ (i // 2)) + i % 2 for i in range(16)]
    ahead = [*range(8), *(8 + i for i in range(tops[-2]))]
    last = [8 + i for i in range(tops[-2], tops[-1])]
    stitched_out = lay(
        jnp.stack([b, *(spots[i] for i in ahead)]), [*st_kept, *st_got[:-1]], None, 8 * rows, piece
    )
    stitched_out = lay(
        jnp.stack([b, *(spots[i] for i in last)]), st_got[-1:], stitched_out, 8 * rows, piece
    )
    own_s, other_s = s_a[0], s_a[1]
    stitch_grad = jnp.where(tower == 0, jnp.stack([own_s, other_s]), jnp.stack([other_s, own_s]))
    return (
        stitched_out[None],
        acts_grad[None],
        weight_grad[None],
        s_a[2][None],
        stitch_grad[None],
    )


def solution(mesh):
    placed = (
        P("tower", ("batch", "mp"), None),
        P("tower", None, "mp"),
        P("tower", "mp"),
        P("tower", None, "mp"),
        P("tower", "batch", "mp"),
        P("batch"),
        P("batch"),
        P("batch"),
    )
    per_device = squares if mesh.shape["mp"] == 8 and mesh.shape["batch"] == 2 else general
    return jax.shard_map(
        per_device,
        mesh=mesh,
        in_specs=placed,
        out_specs=(
            P("tower", "batch", "mp"),
            P("tower", ("batch", "mp"), None),
            P("tower", None, "mp"),
            P("tower", "mp"),
            P("tower", None, "mp"),
        ),
        check_vma=False,
    )
```

```python
import functools

import jax
import jax.numpy as jnp
from jax import lax
from jax.experimental import pallas as pl
from jax.experimental.pallas import tpu as pltpu
from jax.sharding import PartitionSpec as P

BF = jnp.bfloat16
F32 = jnp.float32


def swapped(block, axis, mask):
    count = lax.axis_size(axis)
    return lax.ppermute(block, axis, [(i, i ^ mask) for i in range(count)])


def general(acts, fc_weight, fc_bias, stitch, image_grad, crop_counts, row_image, row_live):
    feature_rows = acts[0]
    weight_matrix = fc_weight[0]
    layer_bias = fc_bias[0].astype(jnp.float32)
    coefs = stitch[0]
    grads_img = image_grad[0]
    gathered = lax.all_gather(feature_rows, "mp", axis=0, tiled=True)
    preactivation = (
        jnp.dot(gathered, weight_matrix, preferred_element_type=jnp.float32) + layer_bias[None, :]
    )
    active = preactivation > 0
    hidden = jnp.maximum(preactivation, 0.0).astype(jnp.bfloat16)
    tower = lax.axis_index("tower")
    self_coefficient = jnp.where(tower == 0, coefs[0], coefs[1])
    other_coef = jnp.where(tower == 0, coefs[1], coefs[0])
    partner = swapped(hidden, "tower", 1)
    hidden_wide = hidden.astype(jnp.float32)
    partner_wide = partner.astype(jnp.float32)
    stitched = self_coefficient[None, :] * hidden_wide + other_coef[None, :] * partner_wide
    live = row_live.astype(jnp.float32)
    stitched_out = (stitched * live[:, None]).astype(jnp.bfloat16)
    img_dev = crop_counts.shape[0]
    local_img = row_image - lax.axis_index("batch") * img_dev
    match = local_img[:, None] == jnp.arange(img_dev, dtype=jnp.int32)[None, :]
    per_row = jnp.sum(jnp.where(match, crop_counts[None, :].astype(jnp.float32), 0.0), axis=1)
    row_weighting_scale = live / per_row
    picked = jnp.dot(match.astype(jnp.bfloat16), grads_img, preferred_element_type=jnp.float32)
    out_grad = (picked * row_weighting_scale[:, None]).astype(jnp.bfloat16)
    out_wide = out_grad.astype(jnp.float32)
    returned = swapped(other_coef[None, :] * out_wide, "tower", 1)
    hidden_grad = (self_coefficient[None, :] * out_wide + returned).astype(jnp.bfloat16)
    pre_grad = jnp.where(active, hidden_grad, jnp.zeros_like(hidden_grad))
    own_stitch = jnp.sum(out_wide * hidden_wide, axis=0)
    other_stitch = jnp.sum(out_wide * partner_wide, axis=0)
    stitch_grad = jnp.where(
        tower == 0, jnp.stack([own_stitch, other_stitch]), jnp.stack([other_stitch, own_stitch])
    )
    bias_grad = jnp.sum(pre_grad.astype(jnp.float32), axis=0)
    weight_grad = lax.dot_general(
        gathered, pre_grad, (((0,), (0,)), ((), ())), preferred_element_type=jnp.float32
    )
    weight_grad, bias_grad, stitch_grad = lax.psum((weight_grad, bias_grad, stitch_grad), "batch")
    input_grad = lax.psum_scatter(
        lax.dot_general(
            pre_grad, weight_matrix, (((1,), (1,)), ((), ())), preferred_element_type=jnp.float32
        ),
        "mp",
        scatter_dimension=0,
        tiled=True,
    )
    return (
        stitched_out[None],
        input_grad.astype(jnp.bfloat16)[None],
        weight_grad[None],
        bias_grad[None],
        stitch_grad[None],
    )

STEPS = (
    "+y0", "+z0", "+o", "o", "z0", "+z1", "+p0", "+d0", "+a", "z1", "+z2", "+d1",
    "p0", "+x0", "+p1", "a", "y0", "d0", "x0", "F01", "p1", "+x1", "+p2", "z2",
    "+d2", "p2", "+x2", "+g", "+m", "x1", "d1", "D02", "x2", "F13", "D23", "d2",
    "g", "m", "+b", "E03", "b",
)

NT = (((1,), (1,)), ((), ()))
TN = (((0,), (0,)), ((), ()))
HEAVY = pl.CostEstimate(flops=1000, bytes_accessed=60000000, transcendentals=0)
LIGHT = pl.CostEstimate(flops=1000, bytes_accessed=1000, transcendentals=0)


def forward_body(n_x, starts, has_acc, *refs):
    xs, rest = refs[:n_x], list(refs[n_x:])
    w_m, w_o = rest.pop(0), rest.pop(0)
    n_q = len(starts) - 1
    ps = [rest.pop(0) for _ in range(n_q)]
    gs = [rest.pop(0) for _ in range(n_q)]
    acc_in = rest.pop(0) if has_acc else None
    out, features, weights = rest
    i = pl.program_id(0)
    half = w_m.shape[1]

    @pl.when(i == 0)
    def _():
        if has_acc:
            out[...] = acc_in[...]
        else:
            out[...] = jnp.zeros_like(out)

    lo = 0
    for x in xs:
        features[lo : lo + x.shape[0], :] = x[...]
        lo += x.shape[0]
    weights[:, :half] = w_m[...]
    weights[:, 2 * half : 3 * half] = w_o[...]
    for q in range(n_q):

        @pl.when((i >= starts[q]) & (i < starts[q + 1]))
        def _():
            weights[:, half : 2 * half] = ps[q][...]
            weights[:, 3 * half :] = gs[q][...]

    out[...] += jnp.dot(features[...], weights[...], preferred_element_type=F32)


def forward(xs, w_m, w_o, ps, gs, lo, block, acc=None):
    starts = [0]
    for p in ps:
        starts.append(starts[-1] + p.shape[0] // block)
    rows = sum(x.shape[0] for x in xs)
    half = w_m.shape[1]
    operands = [*xs, w_m, w_o, *ps, *gs]
    specs = [pl.BlockSpec((x.shape[0], block), lambda i: (0, lo + i)) for x in xs]
    specs += [pl.BlockSpec((block, half), lambda i: (lo + i, 0))] * 2
    for a, e in [*zip(starts, starts[1:])] * 2:
        specs.append(
            pl.BlockSpec((block, half), lambda i, a=a, e=e: (jnp.clip(i - a, 0, e - a - 1), 0))
        )
    wide = pl.BlockSpec((rows, 4 * half), lambda i: (0, 0))
    if acc is not None:
        operands.append(acc)
        specs.append(wide)
    return pl.pallas_call(
        functools.partial(forward_body, len(xs), starts, acc is not None),
        out_shape=jax.ShapeDtypeStruct((rows, 4 * half), F32),
        grid=(starts[-1],),
        in_specs=specs,
        out_specs=wide,
        scratch_shapes=[pltpu.VMEM((rows, block), BF), pltpu.VMEM((block, 4 * half), BF)],
        cost_estimate=LIGHT,
    )(*operands)


def activate_body(bounds, *refs):
    accs, (vec, og_a, og_b, oo_a, oo_b, hid, pre_grad) = refs[: len(bounds)], refs[len(bounds) :]
    i = pl.program_id(0)
    half = og_a.shape[1] // 2
    for acc, (lo, hi) in zip(accs, bounds):

        @pl.when((i >= lo) & (i < hi))
        def _():
            for j in range(4):
                at = slice(j * half, (j + 1) * half)
                part = slice(j // 2 * half, (j // 2 + 1) * half)
                og, oo = (og_b, oo_b) if j % 2 else (og_a, oo_a)
                pre = acc[:, at] + vec[3:4, at]
                hg = vec[0:1, at] * og[:, part].astype(F32) + vec[2:3, at] * oo[:, part].astype(F32)
                hid[:, at] = jnp.maximum(pre, 0.0).astype(BF)
                pre_grad[:, at] = jnp.where(pre > 0, hg.astype(BF), jnp.zeros(hg.shape, BF))


def activate(accs, vec, ogs, rows):
    wide = vec.shape[1]
    total = ogs[0].shape[0]
    bounds, lo = [], 0
    for acc in accs:
        bounds.append((lo, lo + acc.shape[0] // rows))
        lo = bounds[-1][1]
    specs = [
        pl.BlockSpec((rows, wide), lambda i, lo=lo, hi=hi: (jnp.clip(i - lo, 0, hi - lo - 1), 0))
        for lo, hi in bounds
    ]
    specs.append(pl.BlockSpec(vec.shape, lambda i: (0, 0)))
    specs += [pl.BlockSpec((rows, wide // 2), lambda i: (i, 0))] * 4
    at = pl.BlockSpec((rows, wide), lambda i: (i, 0))
    return pl.pallas_call(
        functools.partial(activate_body, bounds),
        out_shape=(jax.ShapeDtypeStruct((total, wide), BF),) * 2,
        grid=(bounds[-1][1],),
        in_specs=specs,
        out_specs=[at, at],
        cost_estimate=LIGHT,
    )(*accs, vec, *ogs)


def nt_body(n_p, n_w, n_add, *refs):
    ps, ws = refs[:n_p], refs[n_p : n_p + n_w]
    adds, out = refs[n_p + n_w : n_p + n_w + n_add], refs[-1]
    weights = jnp.concatenate([w[...] for w in ws], 1)
    rows = ps[0].shape[0]
    for j, p in enumerate(ps):
        r = lax.dot_general(p[...], weights, NT, preferred_element_type=F32)
        for a in adds:
            r = r + a[...].astype(F32)
        out[j * rows : (j + 1) * rows, :] = r.astype(BF)


def nt_product(pre_grad, picks, ws, adds, rows, width, block, into=None, cost=LIGHT):
    steps = width // block
    operands, specs = [], []
    for o in picks:
        operands.append(pre_grad)
        specs.append(pl.BlockSpec((rows, pre_grad.shape[1]), lambda i, o=o: (o, 0)))
    for w, lo in ws:
        operands.append(w)
        specs.append(pl.BlockSpec((block, w.shape[1]), lambda i, lo=lo: (lo + i, 0)))
    for a, r, lo in adds:
        operands.append(a)
        specs.append(pl.BlockSpec((rows, block), lambda i, r=r, lo=lo: (r, lo + i)))
    body = functools.partial(nt_body, len(picks), len(ws), len(adds))
    height = rows * len(picks)
    shape, first, alias = (height, width), 0, {}
    if into is not None:
        held, shape, first = into
        if held is not None:
            alias = {len(operands): 0}
            operands.append(held)
            specs.append(pl.BlockSpec(memory_space=pl.ANY))
            inner = body

            def body(*refs):
                inner(*refs[:-2], refs[-1])

    return pl.pallas_call(
        body,
        out_shape=jax.ShapeDtypeStruct(shape, BF),
        grid=(steps,),
        in_specs=specs,
        out_specs=pl.BlockSpec((height, block), lambda i: (0, first + i)),
        input_output_aliases=alias,
        cost_estimate=cost,
    )(*operands)


def sent_body(n_x, *refs):
    block = jnp.concatenate([x[...] for x in refs[:n_x]], 0)
    p, out = refs[n_x], refs[n_x + 1]
    out[...] = lax.dot_general(block, p[...], TN, preferred_element_type=F32).astype(BF)


def kept_body(n_x, *refs):
    block = jnp.concatenate([x[...] for x in refs[:n_x]], 0)
    p, got, near, far = refs[n_x:]
    r = lax.dot_general(block, p[...], TN, preferred_element_type=F32) + got[...].astype(F32)
    half = near.shape[1]
    near[...] = r[:, :half]
    far[...] = r[:, half:].astype(BF)


def tn_product(xs, pre_grad, side, lo, width, block, got=None):
    cols = pre_grad.shape[1] // 2
    steps = width // block
    operands = [*xs, pre_grad]
    specs = [pl.BlockSpec((x.shape[0], block), lambda i: (0, lo + i)) for x in xs]
    specs.append(pl.BlockSpec((pre_grad.shape[0], cols), lambda i: (0, side)))
    if got is None:
        body = functools.partial(sent_body, len(xs))
        outs = jax.ShapeDtypeStruct((width, cols), BF)
        out_specs = pl.BlockSpec((block, cols), lambda i: (i, 0))
    else:
        body = functools.partial(kept_body, len(xs))
        operands.append(got)
        specs.append(pl.BlockSpec((block, cols), lambda i: (i, 0)))
        half = cols // 2
        outs = (
            jax.ShapeDtypeStruct((width, half), F32),
            jax.ShapeDtypeStruct((width, half), BF),
        )
        out_specs = [pl.BlockSpec((block, half), lambda i: (i, 0))] * 2
    return pl.pallas_call(
        body,
        out_shape=outs,
        grid=(steps,),
        in_specs=specs,
        out_specs=out_specs,
        cost_estimate=LIGHT,
    )(*operands)


def add_body(near, got, out):
    out[...] = (near[...] + got[...].astype(F32)).astype(BF)


def finished(near, got):
    width, half = near.shape
    spec = pl.BlockSpec((width // 2, half), lambda i: (i, 0))
    return pl.pallas_call(
        add_body,
        out_shape=jax.ShapeDtypeStruct((width, half), BF),
        grid=(2,),
        in_specs=[spec, spec],
        out_specs=spec,
        cost_estimate=LIGHT,
    )(near, got)


def place_body(b, near, got, other, *rest):
    out = rest[-1]
    half = near.shape[1]
    total = near[...] + got[...].astype(F32)
    wide = other[...].astype(F32)
    first = b[0] == 0
    out[:, :half] = jnp.where(first, total, wide)
    out[:, half:] = jnp.where(first, wide, total)


def place(b, near, got, other, held, depth, at, cost=LIGHT):
    width, half = near.shape
    spec = pl.BlockSpec((width // 2, half), lambda i, b: (i, 0))
    operands, specs, alias = [near, got, other], [spec] * 3, {}
    if held is not None:
        alias = {4: 0}
        operands.append(held)
        specs.append(pl.BlockSpec(memory_space=pl.ANY))
    return pl.pallas_call(
        place_body,
        out_shape=jax.ShapeDtypeStruct((depth, 2 * half), F32),
        grid_spec=pltpu.PrefetchScalarGridSpec(
            num_scalar_prefetch=1,
            grid=(2,),
            in_specs=specs,
            out_specs=pl.BlockSpec((width // 2, 2 * half), lambda i, b: (2 * at + i, 0)),
        ),
        input_output_aliases=alias,
        cost_estimate=cost,
    )(b, *operands)


def lay(where, pieces, held, height, rows):
    width = pieces[0].shape[1]
    operands, specs, bounds, lo = [], [], [], 0
    for v in pieces:
        n = v.shape[0] // rows
        operands.append(v)
        specs.append(
            pl.BlockSpec((rows, width), lambda i, at, lo=lo, n=n: (jnp.clip(i - lo, 0, n - 1), 0))
        )
        bounds.append((lo, lo + n))
        lo += n
    alias = {}
    if held is not None:
        alias = {len(operands) + 1: 0}
        operands.append(held)
        specs.append(pl.BlockSpec(memory_space=pl.ANY))

    def body(at, *refs):
        out = refs[-1]
        half = width // 2
        i = pl.program_id(0)
        for ref, (a, e) in zip(refs, bounds):

            @pl.when((i >= a) & (i < e))
            def _():
                m, o = ref[:, :half].astype(F32), ref[:, half:].astype(F32)
                first = at[0] == 0
                out[:, :half] = jnp.where(first, m, o).astype(BF)
                out[:, half:] = jnp.where(first, o, m).astype(BF)

    return pl.pallas_call(
        body,
        out_shape=jax.ShapeDtypeStruct((height, width), BF),
        grid_spec=pltpu.PrefetchScalarGridSpec(
            num_scalar_prefetch=1,
            grid=(lo,),
            in_specs=specs,
            out_specs=pl.BlockSpec((rows, width), lambda i, at: (at[i + 1], 0)),
        ),
        input_output_aliases=alias,
        cost_estimate=HEAVY,
    )(where, *operands)


def squares(acts, fc_weight, fc_bias, stitch, image_grad, crop_counts, row_image, row_live):
    x = acts[0]
    w = fc_weight[0]
    rows, depth = x.shape
    cols = w.shape[1]
    half = cols // 2
    me = lax.axis_index("mp")
    b = lax.axis_index("batch")
    tower = lax.axis_index("tower")
    nk = 6
    dk = depth // nk
    wat = (0, 3, 5, 6)
    nw = len(wat) - 1
    block = 512 if dk % 512 == 0 else dk

    token = []

    def tie(v, *deps):
        deps = [d for d in (*deps, *token) if d is not None]
        return lax.optimization_barrier((v, *deps))[0] if deps else v

    def only(v, *deps):
        return lax.optimization_barrier((v, *deps))[0] if deps else v

    def wait(v):
        v = tie(v)
        token[:] = [v]
        return v

    def lane(axis, mask):
        return lambda v, *deps: swapped(tie(v, *deps), axis, mask)

    sy = lane("mp", 1)
    sz = lane("mp", 2)
    sp = lane("mp", 4)
    sx = lane("batch", 1)
    st = lane("tower", 1)

    def mine(v):
        return lax.dynamic_slice_in_dim(v, b * half, half, v.ndim - 1)

    def other(v):
        return lax.dynamic_slice_in_dim(v, (1 - b) * half, half, v.ndim - 1)

    def natural(m, o):
        return jnp.where(b == 0, jnp.concatenate([m, o], -1), jnp.concatenate([o, m], -1))

    def four(a, c):
        return jnp.concatenate([a[..., :half], c[..., :half], a[..., half:], c[..., half:]], -1)

    def third(v, q):
        return v[wat[q] * dk : wat[q + 1] * dk]

    w_m = mine(w)
    w_o = other(w)
    coefs = stitch[0]
    self_c = jnp.where(tower == 0, coefs[0], coefs[1])
    other_c = jnp.where(tower == 0, coefs[1], coefs[0])
    grads = image_grad[0]
    grads = jnp.concatenate([mine(grads), other(grads)], 1)

    def square_rows(v):
        v = v.reshape(-1, rows)
        return jnp.concatenate(
            [lax.dynamic_index_in_dim(v, me ^ o, 0, keepdims=False) for o in range(4)], 0
        )

    live = square_rows(row_live).astype(F32)
    img_dev = crop_counts.shape[0]
    local_img = square_rows(row_image) - b * img_dev
    match = local_img[:, None] == jnp.arange(img_dev, dtype=jnp.int32)[None, :]
    per_row = jnp.sum(jnp.where(match, crop_counts[None, :].astype(F32), 0.0), axis=1)
    scale = live / per_row

    def out_grad_of(g):
        picked = jnp.dot(match.astype(BF), g, preferred_element_type=F32)
        return (picked * scale[:, None]).astype(BF)

    zat = [c * rows // 384 for c in (0, 128, 256, 384)]
    nz = len(zat) - 1
    rz = rows - zat[-2]
    first = x[: zat[1]]
    late = lax.optimization_barrier((x, first))[0]
    V = {"X": x, "G": grads, "oc0": other_c}
    for i in range(nz):
        V[f"Z{i}"] = first if i == 0 else late[zat[i] : zat[i + 1]]
    for q in range(nw):
        V[f"W{q}"] = third(w_m, q)
    fb = dk
    send = {"z": (sz, "Z"), "y": (sy, "X"), "d": (sy, "z"), "p": (sp, "W"), "x": (sx, "p")}
    once = {"g": (sp, "G"), "m": (sp, "small"), "o": (st, "oc0"), "a": (st, "oga"), "b": (st, "ogb")}

    def known():
        return [x, V["y0"], *(V[f"z{i}"] for i in range(nz - 1))]

    def weight_parts(q0, q1):
        ps = [V[f"p{q}"] for q in range(q0, q1)]
        return ps, [V[f"x{q}"] for q in range(q0, q1)], wat[q0], fb

    for step in STEPS:
        if step[0] == "+":
            key = step[1:]
            if key == "y0":
                V[key] = sy(x)
                continue
            if key in once:
                if key == "o":
                    names = [n for n in V if n[0] in "ZW" and n != "Z0"]
                    cut = lax.optimization_barrier((other_c, *(V[n] for n in names)))
                    V.update(zip(["oc0", *names], cut))
                elif key == "m":
                    small = jnp.stack([self_c, other_c, V["o"], fc_bias[0].astype(F32)])
                    V["small"] = jnp.concatenate([mine(small), other(small)], 1)
                elif key == "a":
                    V["oga"] = out_grad_of(grads)
                elif key == "b":
                    V["ogb"] = out_grad_of(V["g"])
                f, src = once[key]
                V[key] = f(V[src])
            else:
                f, src = send[key[0]]
                V[key] = f(V[src + key[1:]])
        elif step[0] == "F":
            q0, q1 = int(step[1]), int(step[2])
            xs = known()
            xs[0] = tie(xs[0])
            V["F"] = forward(xs, w_m, w_o, *weight_parts(q0, q1), V.get("F"))
            token[:] = [V["F"]]
        elif step[0] in "DE":
            q0, q1 = int(step[1]), int(step[2])
            rest = [V[f"d{nz - 1}"]]
            if step[0] == "D":
                rest = [V[f"z{nz - 1}"], *(V[f"d{i}"] for i in range(nz - 1))]
            rest[0] = tie(rest[0])
            V[step[0]] = forward(rest, w_m, w_o, *weight_parts(q0, q1), V.get(step[0]))
            token[:] = [V[step[0]]]
        else:
            V[step] = wait(V[step])
    p = [V[f"p{q}"] for q in range(nw)]
    xg = [V[f"x{q}"] for q in range(nw)]
    vec = four(V["small"], V["m"])
    self4, other4 = vec[0], vec[1]
    ogs = [V[n] for n in ("oga", "ogb", "a", "b")]
    hidden, pre_grad = activate([V["F"], V["D"], V["E"]], vec, ogs, rz)
    features = [*known(), V[f"z{nz - 1}"], *(V[f"d{i}"] for i in range(nz))]
    per = dk // block

    def weights(c):
        q = max(i for i in range(nw) if wat[i] <= c)
        lo = (c - wat[q]) * per
        return [(w_m, c * per), (p[q], lo), (w_o, c * per), (xg[q], lo)]

    def y_part(c, *deps):
        return nt_product(only(pre_grad, *deps), (1, 3), weights(c), (), rows, dk, block)

    def z_part(c, *deps):
        g = only(pre_grad, *deps)
        return nt_product(g, (2,), weights(c), [(yy[c], 1, 0)], rows, dk, block)

    def own_part(c, held, *deps):
        into = (held, (rows, depth), c * per)
        g = only(pre_grad, *deps)
        return nt_product(
            g, (0,), weights(c), [(yy[c], 0, 0), (zz[c], 0, 0)], rows, dk, block, into,
            HEAVY if c == nk - 1 else LIGHT,
        )

    def dw_sent(c, *deps):
        return tn_product(features, only(pre_grad, *deps), 1, c * per, dk, block)

    def dw_kept(c):
        return tn_product(features, pre_grad, 0, c * per, dk, block, s[c])

    token.clear()
    bvec = jnp.full((1,), b, jnp.int32)

    s, k, a, t, k_got = ([None] * nk for _ in range(5))
    yy, zz, own, put = ([None] * nk for _ in range(4))

    hid_other = None
    later = {}

    def do_sums():
        hw, how = hidden.astype(F32), hid_other.astype(F32)
        sums = jnp.stack(
            [
                jnp.sum(out_wide * hw, axis=0),
                jnp.sum(out_wide * how, axis=0),
                jnp.sum(pre_grad.astype(F32), axis=0),
            ]
        )
        later["a"] = jnp.concatenate([sums[:, :half], sums[:, cols : cols + half]], 1)
        s_b = jnp.concatenate([sums[:, half:cols], sums[:, cols + half :]], 1)
        later["p"] = sp(s_b)

    def do_st():
        hw, how = hidden.astype(F32), hid_other.astype(F32)
        stitched = ((self4[None] * hw + other4[None] * how) * live[:, None]).astype(BF)
        later["st_a"] = jnp.concatenate([stitched[:, :half], stitched[:, cols : cols + half]], 1)
        st_b = jnp.concatenate([stitched[:, half:cols], stitched[:, cols + half :]], 1)
        later["st"] = sp(st_b)

    def do_sumx():
        s_a = later["a"] + later["p"]
        s_a = natural(s_a[:, :half], s_a[:, half:])
        later["s"] = s_a + sx(s_a)

    def lump(n, *extra):
        places = [(v, c) for v, c in ((yy, n), (s, n), (zz, n - 1), (k_got, n - 1), (a, n - 2))
                  if 0 <= c < nk and v[c] is not None]
        outs = lax.optimization_barrier((*(v[c] for v, c in places), *extra))
        for (v, c), o in zip(places, outs):
            v[c] = o
        held = [v[c] for v, c in ((own, n - 2), (put, n - 3)) if 0 <= c < nk]
        token[:] = [*outs, *held]
        return outs[len(places):]

    def st_piece(half_rows):
        lo, hi = half_rows
        hw, how = hidden[lo:hi].astype(F32), hid_other[lo:hi].astype(F32)
        stitched = (self4[None] * hw + other4[None] * how) * live[lo:hi, None]
        stitched = stitched.astype(BF)
        kept = jnp.concatenate([stitched[:, :half], stitched[:, cols : cols + half]], 1)
        sent = jnp.concatenate([stitched[:, half:cols], stitched[:, cols + half :]], 1)
        return kept, sp(sent)

    y_next, s_next = y_part(0), None
    cuts = [c * rows // 384 for c in (0, 960, 1536)]
    st_kept, st_got = [], []
    for n in range(nk + 2):
        if n < nk:
            yy[n] = sy(y_next, s_next)
            if n == 0:
                s_next = dw_sent(0, y_next)
            s[n] = sx(s_next)
        extra = []
        if n == 0:
            hid_other = st(only(hidden, y_next))
            out_wide = four(only(V["oga"], s_next), V["ogb"]).astype(F32)
            do_sums()
        if n in (0, 7):
            piece = (0, 7).index(n)
            kept, got_st = st_piece((cuts[piece], cuts[piece + 1]))
            st_kept.append(kept)
            if n == nk + 1:
                st_got.append(got_st)
            else:
                extra.append(got_st)
        if 0 < n <= nk:
            zz[n - 1] = sz(z_part(n - 1))
            t[n - 1], k[n - 1] = dw_kept(n - 1)
            k_got[n - 1] = sp(k[n - 1])
        if n == 0:
            extra = [later["p"], *extra]
        if n == 1:
            do_sumx()
            extra = [later["s"]]
        if 1 < n:
            a[n - 2] = sx(finished(t[n - 2], k_got[n - 2]))
            own[n - 2] = own_part(n - 2, own[n - 3] if n > 2 else None)
        if 2 < n:
            put[n - 3] = place(
                bvec, t[n - 3], k_got[n - 3], a[n - 3], put[n - 4] if n > 3 else None, depth, n - 3,
                HEAVY if n == nk + 1 else LIGHT,
            )
        if n + 1 < nk:
            y_next, s_next = y_part(n + 1), dw_sent(n + 1)
        outs = lump(n, *extra)
        if n == 0:
            later["p"], *outs = outs
        if n == 1:
            later["s"], *outs = outs
        st_got += outs
    token.clear()
    put[-1] = place(bvec, t[-1], k_got[-1], a[-1], put[-2], depth, nk - 1)
    held_x, held_w = own[-1], put[-1]
    s_a = later["s"]
    acts_grad, weight_grad = held_x, held_w

    piece = rows // 2
    tops = [lo // piece for lo in cuts]
    spots = [2 * (me ^ (i // 2)) + i % 2 for i in range(16)]
    ahead = [*range(8), *(8 + i for i in range(tops[-2]))]
    last = [8 + i for i in range(tops[-2], tops[-1])]
    stitched_out = lay(
        jnp.stack([b, *(spots[i] for i in ahead)]), [*st_kept, *st_got[:-1]], None, 8 * rows, piece
    )
    stitched_out = lay(
        jnp.stack([b, *(spots[i] for i in last)]), st_got[-1:], stitched_out, 8 * rows, piece
    )
    own_s, other_s = s_a[0], s_a[1]
    stitch_grad = jnp.where(tower == 0, jnp.stack([own_s, other_s]), jnp.stack([other_s, own_s]))
    return (
        stitched_out[None],
        acts_grad[None],
        weight_grad[None],
        s_a[2][None],
        stitch_grad[None],
    )


def solution(mesh):
    placed = (
        P("tower", ("batch", "mp"), None),
        P("tower", None, "mp"),
        P("tower", "mp"),
        P("tower", None, "mp"),
        P("tower", "batch", "mp"),
        P("batch"),
        P("batch"),
        P("batch"),
    )
    per_device = squares if mesh.shape["mp"] == 8 and mesh.shape["batch"] == 2 else general
    return jax.shard_map(
        per_device,
        mesh=mesh,
        in_specs=placed,
        out_specs=(
            P("tower", "batch", "mp"),
            P("tower", ("batch", "mp"), None),
            P("tower", None, "mp"),
            P("tower", "mp"),
            P("tower", None, "mp"),
        ),
        check_vma=False,
    )
```

```python
import functools

import jax
import jax.numpy as jnp
from jax import lax
from jax.experimental import pallas as pl
from jax.experimental.pallas import tpu as pltpu
from jax.sharding import PartitionSpec as P

BF = jnp.bfloat16
F32 = jnp.float32


def swapped(block, axis, mask):
    count = lax.axis_size(axis)
    return lax.ppermute(block, axis, [(i, i ^ mask) for i in range(count)])


def general(acts, fc_weight, fc_bias, stitch, image_grad, crop_counts, row_image, row_live):
    feature_rows = acts[0]
    weight_matrix = fc_weight[0]
    layer_bias = fc_bias[0].astype(jnp.float32)
    coefs = stitch[0]
    grads_img = image_grad[0]
    gathered = lax.all_gather(feature_rows, "mp", axis=0, tiled=True)
    preactivation = (
        jnp.dot(gathered, weight_matrix, preferred_element_type=jnp.float32) + layer_bias[None, :]
    )
    active = preactivation > 0
    hidden = jnp.maximum(preactivation, 0.0).astype(jnp.bfloat16)
    tower = lax.axis_index("tower")
    self_coefficient = jnp.where(tower == 0, coefs[0], coefs[1])
    other_coef = jnp.where(tower == 0, coefs[1], coefs[0])
    partner = swapped(hidden, "tower", 1)
    hidden_wide = hidden.astype(jnp.float32)
    partner_wide = partner.astype(jnp.float32)
    stitched = self_coefficient[None, :] * hidden_wide + other_coef[None, :] * partner_wide
    live = row_live.astype(jnp.float32)
    stitched_out = (stitched * live[:, None]).astype(jnp.bfloat16)
    img_dev = crop_counts.shape[0]
    local_img = row_image - lax.axis_index("batch") * img_dev
    match = local_img[:, None] == jnp.arange(img_dev, dtype=jnp.int32)[None, :]
    per_row = jnp.sum(jnp.where(match, crop_counts[None, :].astype(jnp.float32), 0.0), axis=1)
    row_weighting_scale = live / per_row
    picked = jnp.dot(match.astype(jnp.bfloat16), grads_img, preferred_element_type=jnp.float32)
    out_grad = (picked * row_weighting_scale[:, None]).astype(jnp.bfloat16)
    out_wide = out_grad.astype(jnp.float32)
    returned = swapped(other_coef[None, :] * out_wide, "tower", 1)
    hidden_grad = (self_coefficient[None, :] * out_wide + returned).astype(jnp.bfloat16)
    pre_grad = jnp.where(active, hidden_grad, jnp.zeros_like(hidden_grad))
    own_stitch = jnp.sum(out_wide * hidden_wide, axis=0)
    other_stitch = jnp.sum(out_wide * partner_wide, axis=0)
    stitch_grad = jnp.where(
        tower == 0, jnp.stack([own_stitch, other_stitch]), jnp.stack([other_stitch, own_stitch])
    )
    bias_grad = jnp.sum(pre_grad.astype(jnp.float32), axis=0)
    weight_grad = lax.dot_general(
        gathered, pre_grad, (((0,), (0,)), ((), ())), preferred_element_type=jnp.float32
    )
    weight_grad, bias_grad, stitch_grad = lax.psum((weight_grad, bias_grad, stitch_grad), "batch")
    input_grad = lax.psum_scatter(
        lax.dot_general(
            pre_grad, weight_matrix, (((1,), (1,)), ((), ())), preferred_element_type=jnp.float32
        ),
        "mp",
        scatter_dimension=0,
        tiled=True,
    )
    return (
        stitched_out[None],
        input_grad.astype(jnp.bfloat16)[None],
        weight_grad[None],
        bias_grad[None],
        stitch_grad[None],
    )

STEPS = (
    "+y0", "+z0", "+o", "o", "z0", "+z1", "+p0", "+d0", "+a", "z1", "+z2", "+d1",
    "p0", "+x0", "+p1", "a", "y0", "d0", "x0", "F01", "p1", "+x1", "+p2", "z2",
    "+d2", "p2", "+x2", "+g", "+m", "x1", "d1", "D02", "x2", "F13", "D23", "d2",
    "g", "m", "+b", "E03", "b",
)

NT = (((1,), (1,)), ((), ()))
TN = (((0,), (0,)), ((), ()))
HEAVY = pl.CostEstimate(flops=1000, bytes_accessed=60000000, transcendentals=0)
LIGHT = pl.CostEstimate(flops=1000, bytes_accessed=1000, transcendentals=0)


def forward_body(n_x, starts, has_acc, *refs):
    xs, rest = refs[:n_x], list(refs[n_x:])
    w_m, w_o = rest.pop(0), rest.pop(0)
    n_q = len(starts) - 1
    ps = [rest.pop(0) for _ in range(n_q)]
    gs = [rest.pop(0) for _ in range(n_q)]
    acc_in = rest.pop(0) if has_acc else None
    out = rest[0]
    i = pl.program_id(0)
    half = w_m.shape[1]

    @pl.when(i == 0)
    def _():
        if has_acc:
            out[...] = acc_in[...]
        else:
            out[...] = jnp.zeros_like(out)

    for q in range(n_q):

        @pl.when((i >= starts[q]) & (i < starts[q + 1]))
        def _():
            lo = 0
            for x in xs:
                rows = x.shape[0]
                for j, w in enumerate((w_m, ps[q], w_o, gs[q])):
                    out[lo : lo + rows, j * half : (j + 1) * half] += jnp.dot(
                        x[...], w[...], preferred_element_type=F32
                    )
                lo += rows


def forward(xs, w_m, w_o, ps, gs, lo, block, acc=None):
    starts = [0]
    for p in ps:
        starts.append(starts[-1] + p.shape[0] // block)
    rows = sum(x.shape[0] for x in xs)
    half = w_m.shape[1]
    operands = [*xs, w_m, w_o, *ps, *gs]
    specs = [pl.BlockSpec((x.shape[0], block), lambda i: (0, lo + i)) for x in xs]
    specs += [pl.BlockSpec((block, half), lambda i: (lo + i, 0))] * 2
    for a, e in [*zip(starts, starts[1:])] * 2:
        specs.append(
            pl.BlockSpec((block, half), lambda i, a=a, e=e: (jnp.clip(i - a, 0, e - a - 1), 0))
        )
    wide = pl.BlockSpec((rows, 4 * half), lambda i: (0, 0))
    if acc is not None:
        operands.append(acc)
        specs.append(wide)
    return pl.pallas_call(
        functools.partial(forward_body, len(xs), starts, acc is not None),
        out_shape=jax.ShapeDtypeStruct((rows, 4 * half), F32),
        grid=(starts[-1],),
        in_specs=specs,
        out_specs=wide,
        cost_estimate=LIGHT,
    )(*operands)


def activate_body(bounds, *refs):
    accs, (vec, og_a, og_b, oo_a, oo_b, hid, pre_grad) = refs[: len(bounds)], refs[len(bounds) :]
    i = pl.program_id(0)
    half = og_a.shape[1] // 2
    for acc, (lo, hi) in zip(accs, bounds):

        @pl.when((i >= lo) & (i < hi))
        def _():
            for j in range(4):
                at = slice(j * half, (j + 1) * half)
                part = slice(j // 2 * half, (j // 2 + 1) * half)
                og, oo = (og_b, oo_b) if j % 2 else (og_a, oo_a)
                pre = acc[:, at] + vec[3:4, at]
                hg = vec[0:1, at] * og[:, part].astype(F32) + vec[2:3, at] * oo[:, part].astype(F32)
                hid[:, at] = jnp.maximum(pre, 0.0).astype(BF)
                pre_grad[:, at] = jnp.where(pre > 0, hg.astype(BF), jnp.zeros(hg.shape, BF))


def activate(accs, vec, ogs, rows):
    wide = vec.shape[1]
    total = ogs[0].shape[0]
    bounds, lo = [], 0
    for acc in accs:
        bounds.append((lo, lo + acc.shape[0] // rows))
        lo = bounds[-1][1]
    specs = [
        pl.BlockSpec((rows, wide), lambda i, lo=lo, hi=hi: (jnp.clip(i - lo, 0, hi - lo - 1), 0))
        for lo, hi in bounds
    ]
    specs.append(pl.BlockSpec(vec.shape, lambda i: (0, 0)))
    specs += [pl.BlockSpec((rows, wide // 2), lambda i: (i, 0))] * 4
    at = pl.BlockSpec((rows, wide), lambda i: (i, 0))
    return pl.pallas_call(
        functools.partial(activate_body, bounds),
        out_shape=(jax.ShapeDtypeStruct((total, wide), BF),) * 2,
        grid=(bounds[-1][1],),
        in_specs=specs,
        out_specs=[at, at],
        cost_estimate=LIGHT,
    )(*accs, vec, *ogs)


def nt_body(n_p, n_w, n_add, *refs):
    ps, ws = refs[:n_p], refs[n_p : n_p + n_w]
    adds, out = refs[n_p + n_w : n_p + n_w + n_add], refs[-1]
    weights = jnp.concatenate([w[...] for w in ws], 1)
    rows = ps[0].shape[0]
    for j, p in enumerate(ps):
        r = lax.dot_general(p[...], weights, NT, preferred_element_type=F32)
        for a in adds:
            r = r + a[...].astype(F32)
        out[j * rows : (j + 1) * rows, :] = r.astype(BF)


def nt_product(pre_grad, picks, ws, adds, rows, width, block, into=None, cost=LIGHT):
    steps = width // block
    operands, specs = [], []
    for o in picks:
        operands.append(pre_grad)
        specs.append(pl.BlockSpec((rows, pre_grad.shape[1]), lambda i, o=o: (o, 0)))
    for w, lo in ws:
        operands.append(w)
        specs.append(pl.BlockSpec((block, w.shape[1]), lambda i, lo=lo: (lo + i, 0)))
    for a, r, lo in adds:
        operands.append(a)
        specs.append(pl.BlockSpec((rows, block), lambda i, r=r, lo=lo: (r, lo + i)))
    body = functools.partial(nt_body, len(picks), len(ws), len(adds))
    height = rows * len(picks)
    shape, first, alias = (height, width), 0, {}
    if into is not None:
        held, shape, first = into
        if held is not None:
            alias = {len(operands): 0}
            operands.append(held)
            specs.append(pl.BlockSpec(memory_space=pl.ANY))
            inner = body

            def body(*refs):
                inner(*refs[:-2], refs[-1])

    return pl.pallas_call(
        body,
        out_shape=jax.ShapeDtypeStruct(shape, BF),
        grid=(steps,),
        in_specs=specs,
        out_specs=pl.BlockSpec((height, block), lambda i: (0, first + i)),
        input_output_aliases=alias,
        cost_estimate=cost,
    )(*operands)


def sent_body(n_x, *refs):
    block = jnp.concatenate([x[...] for x in refs[:n_x]], 0)
    p, out = refs[n_x], refs[n_x + 1]
    out[...] = lax.dot_general(block, p[...], TN, preferred_element_type=F32).astype(BF)


def kept_body(n_x, *refs):
    block = jnp.concatenate([x[...] for x in refs[:n_x]], 0)
    p, got, near, far = refs[n_x:]
    r = lax.dot_general(block, p[...], TN, preferred_element_type=F32) + got[...].astype(F32)
    half = near.shape[1]
    near[...] = r[:, :half]
    far[...] = r[:, half:].astype(BF)


def tn_product(xs, pre_grad, side, lo, width, block, got=None):
    cols = pre_grad.shape[1] // 2
    steps = width // block
    operands = [*xs, pre_grad]
    specs = [pl.BlockSpec((x.shape[0], block), lambda i: (0, lo + i)) for x in xs]
    specs.append(pl.BlockSpec((pre_grad.shape[0], cols), lambda i: (0, side)))
    if got is None:
        body = functools.partial(sent_body, len(xs))
        outs = jax.ShapeDtypeStruct((width, cols), BF)
        out_specs = pl.BlockSpec((block, cols), lambda i: (i, 0))
    else:
        body = functools.partial(kept_body, len(xs))
        operands.append(got)
        specs.append(pl.BlockSpec((block, cols), lambda i: (i, 0)))
        half = cols // 2
        outs = (
            jax.ShapeDtypeStruct((width, half), F32),
            jax.ShapeDtypeStruct((width, half), BF),
        )
        out_specs = [pl.BlockSpec((block, half), lambda i: (i, 0))] * 2
    return pl.pallas_call(
        body,
        out_shape=outs,
        grid=(steps,),
        in_specs=specs,
        out_specs=out_specs,
        cost_estimate=LIGHT,
    )(*operands)


def add_body(near, got, out):
    out[...] = (near[...] + got[...].astype(F32)).astype(BF)


def finished(near, got):
    width, half = near.shape
    spec = pl.BlockSpec((width // 2, half), lambda i: (i, 0))
    return pl.pallas_call(
        add_body,
        out_shape=jax.ShapeDtypeStruct((width, half), BF),
        grid=(2,),
        in_specs=[spec, spec],
        out_specs=spec,
        cost_estimate=LIGHT,
    )(near, got)


def place_body(b, near, got, other, *rest):
    out = rest[-1]
    half = near.shape[1]
    total = near[...] + got[...].astype(F32)
    wide = other[...].astype(F32)
    first = b[0] == 0
    out[:, :half] = jnp.where(first, total, wide)
    out[:, half:] = jnp.where(first, wide, total)


def place(b, near, got, other, held, depth, at, cost=LIGHT):
    width, half = near.shape
    spec = pl.BlockSpec((width // 2, half), lambda i, b: (i, 0))
    operands, specs, alias = [near, got, other], [spec] * 3, {}
    if held is not None:
        alias = {4: 0}
        operands.append(held)
        specs.append(pl.BlockSpec(memory_space=pl.ANY))
    return pl.pallas_call(
        place_body,
        out_shape=jax.ShapeDtypeStruct((depth, 2 * half), F32),
        grid_spec=pltpu.PrefetchScalarGridSpec(
            num_scalar_prefetch=1,
            grid=(2,),
            in_specs=specs,
            out_specs=pl.BlockSpec((width // 2, 2 * half), lambda i, b: (2 * at + i, 0)),
        ),
        input_output_aliases=alias,
        cost_estimate=cost,
    )(b, *operands)


def lay(where, pieces, held, height, rows):
    width = pieces[0].shape[1]
    operands, specs, bounds, lo = [], [], [], 0
    for v in pieces:
        n = v.shape[0] // rows
        operands.append(v)
        specs.append(
            pl.BlockSpec((rows, width), lambda i, at, lo=lo, n=n: (jnp.clip(i - lo, 0, n - 1), 0))
        )
        bounds.append((lo, lo + n))
        lo += n
    alias = {}
    if held is not None:
        alias = {len(operands) + 1: 0}
        operands.append(held)
        specs.append(pl.BlockSpec(memory_space=pl.ANY))

    def body(at, *refs):
        out = refs[-1]
        half = width // 2
        i = pl.program_id(0)
        for ref, (a, e) in zip(refs, bounds):

            @pl.when((i >= a) & (i < e))
            def _():
                m, o = ref[:, :half].astype(F32), ref[:, half:].astype(F32)
                first = at[0] == 0
                out[:, :half] = jnp.where(first, m, o).astype(BF)
                out[:, half:] = jnp.where(first, o, m).astype(BF)

    return pl.pallas_call(
        body,
        out_shape=jax.ShapeDtypeStruct((height, width), BF),
        grid_spec=pltpu.PrefetchScalarGridSpec(
            num_scalar_prefetch=1,
            grid=(lo,),
            in_specs=specs,
            out_specs=pl.BlockSpec((rows, width), lambda i, at: (at[i + 1], 0)),
        ),
        input_output_aliases=alias,
        cost_estimate=HEAVY,
    )(where, *operands)


def squares(acts, fc_weight, fc_bias, stitch, image_grad, crop_counts, row_image, row_live):
    x = acts[0]
    w = fc_weight[0]
    rows, depth = x.shape
    cols = w.shape[1]
    half = cols // 2
    me = lax.axis_index("mp")
    b = lax.axis_index("batch")
    tower = lax.axis_index("tower")
    nk = 6
    dk = depth // nk
    wat = (0, 3, 5, 6)
    nw = len(wat) - 1
    block = 512 if dk % 512 == 0 else dk

    token = []

    def tie(v, *deps):
        deps = [d for d in (*deps, *token) if d is not None]
        return lax.optimization_barrier((v, *deps))[0] if deps else v

    def only(v, *deps):
        return lax.optimization_barrier((v, *deps))[0] if deps else v

    def wait(v):
        v = tie(v)
        token[:] = [v]
        return v

    def lane(axis, mask):
        return lambda v, *deps: swapped(tie(v, *deps), axis, mask)

    sy = lane("mp", 1)
    sz = lane("mp", 2)
    sp = lane("mp", 4)
    sx = lane("batch", 1)
    st = lane("tower", 1)

    def mine(v):
        return lax.dynamic_slice_in_dim(v, b * half, half, v.ndim - 1)

    def other(v):
        return lax.dynamic_slice_in_dim(v, (1 - b) * half, half, v.ndim - 1)

    def natural(m, o):
        return jnp.where(b == 0, jnp.concatenate([m, o], -1), jnp.concatenate([o, m], -1))

    def four(a, c):
        return jnp.concatenate([a[..., :half], c[..., :half], a[..., half:], c[..., half:]], -1)

    def third(v, q):
        return v[wat[q] * dk : wat[q + 1] * dk]

    w_m = mine(w)
    w_o = other(w)
    coefs = stitch[0]
    self_c = jnp.where(tower == 0, coefs[0], coefs[1])
    other_c = jnp.where(tower == 0, coefs[1], coefs[0])
    grads = image_grad[0]
    grads = jnp.concatenate([mine(grads), other(grads)], 1)

    def square_rows(v):
        v = v.reshape(-1, rows)
        return jnp.concatenate(
            [lax.dynamic_index_in_dim(v, me ^ o, 0, keepdims=False) for o in range(4)], 0
        )

    live = square_rows(row_live).astype(F32)
    img_dev = crop_counts.shape[0]
    local_img = square_rows(row_image) - b * img_dev
    match = local_img[:, None] == jnp.arange(img_dev, dtype=jnp.int32)[None, :]
    per_row = jnp.sum(jnp.where(match, crop_counts[None, :].astype(F32), 0.0), axis=1)
    scale = live / per_row

    def out_grad_of(g):
        picked = jnp.dot(match.astype(BF), g, preferred_element_type=F32)
        return (picked * scale[:, None]).astype(BF)

    zat = [c * rows // 384 for c in (0, 128, 256, 384)]
    nz = len(zat) - 1
    rz = rows - zat[-2]
    first = x[: zat[1]]
    late = lax.optimization_barrier((x, first))[0]
    V = {"X": x, "G": grads, "oc0": other_c}
    for i in range(nz):
        V[f"Z{i}"] = first if i == 0 else late[zat[i] : zat[i + 1]]
    for q in range(nw):
        V[f"W{q}"] = third(w_m, q)
    fb = dk
    send = {"z": (sz, "Z"), "y": (sy, "X"), "d": (sy, "z"), "p": (sp, "W"), "x": (sx, "p")}
    once = {"g": (sp, "G"), "m": (sp, "small"), "o": (st, "oc0"), "a": (st, "oga"), "b": (st, "ogb")}

    def known():
        return [x, V["y0"], *(V[f"z{i}"] for i in range(nz - 1))]

    def weight_parts(q0, q1):
        ps = [V[f"p{q}"] for q in range(q0, q1)]
        return ps, [V[f"x{q}"] for q in range(q0, q1)], wat[q0], fb

    for step in STEPS:
        if step[0] == "+":
            key = step[1:]
            if key == "y0":
                V[key] = sy(x)
                continue
            if key in once:
                if key == "o":
                    names = [n for n in V if n[0] in "ZW" and n != "Z0"]
                    cut = lax.optimization_barrier((other_c, *(V[n] for n in names)))
                    V.update(zip(["oc0", *names], cut))
                elif key == "m":
                    small = jnp.stack([self_c, other_c, V["o"], fc_bias[0].astype(F32)])
                    V["small"] = jnp.concatenate([mine(small), other(small)], 1)
                elif key == "a":
                    V["oga"] = out_grad_of(grads)
                elif key == "b":
                    V["ogb"] = out_grad_of(V["g"])
                f, src = once[key]
                V[key] = f(V[src])
            else:
                f, src = send[key[0]]
                V[key] = f(V[src + key[1:]])
        elif step[0] == "F":
            q0, q1 = int(step[1]), int(step[2])
            xs = known()
            xs[0] = tie(xs[0])
            V["F"] = forward(xs, w_m, w_o, *weight_parts(q0, q1), V.get("F"))
            token[:] = [V["F"]]
        elif step[0] in "DE":
            q0, q1 = int(step[1]), int(step[2])
            rest = [V[f"d{nz - 1}"]]
            if step[0] == "D":
                rest = [V[f"z{nz - 1}"], *(V[f"d{i}"] for i in range(nz - 1))]
            rest[0] = tie(rest[0])
            V[step[0]] = forward(rest, w_m, w_o, *weight_parts(q0, q1), V.get(step[0]))
            token[:] = [V[step[0]]]
        else:
            V[step] = wait(V[step])
    p = [V[f"p{q}"] for q in range(nw)]
    xg = [V[f"x{q}"] for q in range(nw)]
    vec = four(V["small"], V["m"])
    self4, other4 = vec[0], vec[1]
    ogs = [V[n] for n in ("oga", "ogb", "a", "b")]
    hidden, pre_grad = activate([V["F"], V["D"], V["E"]], vec, ogs, rz)
    features = [*known(), V[f"z{nz - 1}"], *(V[f"d{i}"] for i in range(nz))]
    per = dk // block

    def weights(c):
        q = max(i for i in range(nw) if wat[i] <= c)
        lo = (c - wat[q]) * per
        return [(w_m, c * per), (p[q], lo), (w_o, c * per), (xg[q], lo)]

    def y_part(c, *deps):
        return nt_product(only(pre_grad, *deps), (1, 3), weights(c), (), rows, dk, block)

    def z_part(c, *deps):
        g = only(pre_grad, *deps)
        return nt_product(g, (2,), weights(c), [(yy[c], 1, 0)], rows, dk, block)

    def own_part(c, held, *deps):
        into = (held, (rows, depth), c * per)
        g = only(pre_grad, *deps)
        return nt_product(
            g, (0,), weights(c), [(yy[c], 0, 0), (zz[c], 0, 0)], rows, dk, block, into,
            HEAVY if c == nk - 1 else LIGHT,
        )

    def dw_sent(c, *deps):
        return tn_product(features, only(pre_grad, *deps), 1, c * per, dk, block)

    def dw_kept(c):
        return tn_product(features, pre_grad, 0, c * per, dk, block, s[c])

    token.clear()
    bvec = jnp.full((1,), b, jnp.int32)

    s, k, a, t, k_got = ([None] * nk for _ in range(5))
    yy, zz, own, put = ([None] * nk for _ in range(4))

    hid_other = None
    later = {}

    def do_sums():
        hw, how = hidden.astype(F32), hid_other.astype(F32)
        sums = jnp.stack(
            [
                jnp.sum(out_wide * hw, axis=0),
                jnp.sum(out_wide * how, axis=0),
                jnp.sum(pre_grad.astype(F32), axis=0),
            ]
        )
        later["a"] = jnp.concatenate([sums[:, :half], sums[:, cols : cols + half]], 1)
        s_b = jnp.concatenate([sums[:, half:cols], sums[:, cols + half :]], 1)
        later["p"] = sp(s_b)

    def do_st():
        hw, how = hidden.astype(F32), hid_other.astype(F32)
        stitched = ((self4[None] * hw + other4[None] * how) * live[:, None]).astype(BF)
        later["st_a"] = jnp.concatenate([stitched[:, :half], stitched[:, cols : cols + half]], 1)
        st_b = jnp.concatenate([stitched[:, half:cols], stitched[:, cols + half :]], 1)
        later["st"] = sp(st_b)

    def do_sumx():
        s_a = later["a"] + later["p"]
        s_a = natural(s_a[:, :half], s_a[:, half:])
        later["s"] = s_a + sx(s_a)

    def lump(n, *extra):
        places = [(v, c) for v, c in ((yy, n), (s, n), (zz, n - 1), (k_got, n - 1), (a, n - 2))
                  if 0 <= c < nk and v[c] is not None]
        outs = lax.optimization_barrier((*(v[c] for v, c in places), *extra))
        for (v, c), o in zip(places, outs):
            v[c] = o
        held = [v[c] for v, c in ((own, n - 2), (put, n - 3)) if 0 <= c < nk]
        token[:] = [*outs, *held]
        return outs[len(places):]

    def st_piece(half_rows):
        lo, hi = half_rows
        hw, how = hidden[lo:hi].astype(F32), hid_other[lo:hi].astype(F32)
        stitched = (self4[None] * hw + other4[None] * how) * live[lo:hi, None]
        stitched = stitched.astype(BF)
        kept = jnp.concatenate([stitched[:, :half], stitched[:, cols : cols + half]], 1)
        sent = jnp.concatenate([stitched[:, half:cols], stitched[:, cols + half :]], 1)
        return kept, sp(sent)

    y_next, s_next = y_part(0), None
    cuts = [c * rows // 384 for c in (0, 768, 1536)]
    st_kept, st_got = [], []
    for n in range(nk + 2):
        if n < nk:
            yy[n] = sy(y_next, s_next)
            if n == 0:
                s_next = dw_sent(0, y_next)
            s[n] = sx(s_next)
        extra = []
        if n == 0:
            hid_other = st(only(hidden, y_next))
            out_wide = four(only(V["oga"], s_next), V["ogb"]).astype(F32)
            do_sums()
        if n in (0, 7):
            piece = (0, 7).index(n)
            kept, got_st = st_piece((cuts[piece], cuts[piece + 1]))
            st_kept.append(kept)
            if n == nk + 1:
                st_got.append(got_st)
            else:
                extra.append(got_st)
        if 0 < n <= nk:
            zz[n - 1] = sz(z_part(n - 1))
            t[n - 1], k[n - 1] = dw_kept(n - 1)
            k_got[n - 1] = sp(k[n - 1])
        if n == 0:
            extra = [later["p"], *extra]
        if n == 1:
            do_sumx()
            extra = [later["s"]]
        if 1 < n:
            a[n - 2] = sx(finished(t[n - 2], k_got[n - 2]))
            own[n - 2] = own_part(n - 2, own[n - 3] if n > 2 else None)
        if 2 < n:
            put[n - 3] = place(
                bvec, t[n - 3], k_got[n - 3], a[n - 3], put[n - 4] if n > 3 else None, depth, n - 3,
                HEAVY if n == nk + 1 else LIGHT,
            )
        if n + 1 < nk:
            y_next, s_next = y_part(n + 1), dw_sent(n + 1)
        outs = lump(n, *extra)
        if n == 0:
            later["p"], *outs = outs
        if n == 1:
            later["s"], *outs = outs
        st_got += outs
    token.clear()
    put[-1] = place(bvec, t[-1], k_got[-1], a[-1], put[-2], depth, nk - 1)
    held_x, held_w = own[-1], put[-1]
    s_a = later["s"]
    acts_grad, weight_grad = held_x, held_w

    piece = rows // 2
    tops = [lo // piece for lo in cuts]
    spots = [2 * (me ^ (i // 2)) + i % 2 for i in range(16)]
    ahead = [*range(8), *(8 + i for i in range(tops[-2]))]
    last = [8 + i for i in range(tops[-2], tops[-1])]
    stitched_out = lay(
        jnp.stack([b, *(spots[i] for i in ahead)]), [*st_kept, *st_got[:-1]], None, 8 * rows, piece
    )
    stitched_out = lay(
        jnp.stack([b, *(spots[i] for i in last)]), st_got[-1:], stitched_out, 8 * rows, piece
    )
    own_s, other_s = s_a[0], s_a[1]
    stitch_grad = jnp.where(tower == 0, jnp.stack([own_s, other_s]), jnp.stack([other_s, own_s]))
    return (
        stitched_out[None],
        acts_grad[None],
        weight_grad[None],
        s_a[2][None],
        stitch_grad[None],
    )


def solution(mesh):
    placed = (
        P("tower", ("batch", "mp"), None),
        P("tower", None, "mp"),
        P("tower", "mp"),
        P("tower", None, "mp"),
        P("tower", "batch", "mp"),
        P("batch"),
        P("batch"),
        P("batch"),
    )
    per_device = squares if mesh.shape["mp"] == 8 and mesh.shape["batch"] == 2 else general
    return jax.shard_map(
        per_device,
        mesh=mesh,
        in_specs=placed,
        out_specs=(
            P("tower", "batch", "mp"),
            P("tower", ("batch", "mp"), None),
            P("tower", None, "mp"),
            P("tower", "mp"),
            P("tower", None, "mp"),
        ),
        check_vma=False,
    )
```
